1024 devices in a mesh: dp: 128 (over x, z_hi, y), fsdp: 8 (over z_lo, core).
Axes of the slice: x: 8, y: 8, z: 8 (z_hi: 2, z_lo: 4; z = z_hi * 4 + z_lo), core: 2. Of those that a mesh axis runs over, the one named last changes fastest.
Arguments:
- features: bfloat16 [2048, 14, 14, 1, 512], P(('dp', 'fsdp')), may hold values from -17 to 17
- conv_weight: bfloat16 [1, 4608, 512], P(None, None, 'fsdp'), may hold values from -0.09375 to 0.09375
- proj_weight: bfloat16 [512, 256], replicated, may hold values from -0.5745243 to 0.5745243
- prototypes: bfloat16 [256, 3072], P(None, 'fsdp'), may hold values from -72 to 72
Outputs:
- codes: float32 [2048, 3072], P(('dp', 'fsdp'))
The draws below stay inside these ranges and needn't reach their ends.
All inputs are finite; a program needn't handle non-finite values.
Results may differ from the reference program's by a relative error of at most 0.008.
Values may be sent and summed in bfloat16 or wider, within the bound.
A program may use at most 32 MiB of HBM per device.

```python
import math
import jax
import jax.numpy as jnp
from jax import lax

GW = 512
GROUPS = 1
HW = 14
PROJ = 256
PROTOS = 3072
SINK = 3
IMG_DEV = 2
FEATURE_DEPTH = 512
IMAGES = 2048


def embed_scales(key, top_scale):
    return jnp.exp(jax.random.uniform(jax.random.fold_in(key, 7), (PROJ,), jnp.float32, 0.0, math.log(top_scale)))


def class_of(raw_picks):
    limits = jnp.array([1, 3, 6, 10, 15, 21, 28], jnp.int32)
    return jnp.sum((raw_picks[:, None] >= limits[None, :]).astype(jnp.int32), axis=1)


def channel_blocks():
    return jnp.arange(FEATURE_DEPTH, dtype=jnp.int32) * 8 // FEATURE_DEPTH


def draw_features(key, part):
    key_offset = jax.random.fold_in(key, 11)
    key_level = jax.random.fold_in(key, 12)
    key_noise = jax.random.fold_in(key, 13)
    key_cluster = jax.random.fold_in(key, 14)
    small_shape = (IMAGES, 1, 1, GROUPS, GW)
    full_shape = (IMAGES, HW, HW, GROUPS, GW)
    raw_picks = jax.random.randint(key_cluster, (IMAGES,), 0, 36)
    drift = 3 * jnp.arange(IMAGES, dtype=jnp.int32) // IMAGES
    cluster = (class_of(raw_picks) + drift) % 8
    blocks = channel_blocks().reshape(1, 1, 1, GROUPS, GW)
    active = blocks == cluster.reshape(IMAGES, 1, 1, 1, 1)
    base = 0.7 * jax.random.truncated_normal(key_offset, -3.0, 3.0, small_shape, jnp.float32)
    level = jnp.exp(jax.random.uniform(key_level, small_shape, jnp.float32, -1.0, 1.0))
    noise = jax.random.truncated_normal(key_noise, -4.0, 4.0, full_shape, jnp.float32)
    offset = jnp.where(active, 3.5, base)
    return (offset + level * noise).astype(jnp.bfloat16)


def draw_proj_weight(key, part):
    key_entries = jax.random.fold_in(key, 21)
    shape = (FEATURE_DEPTH, PROJ)
    scales = embed_scales(key, 10.0)
    entries = jax.random.truncated_normal(key_entries, -4.0, 4.0, shape, jnp.float32)
    directions = jax.random.truncated_normal(jax.random.fold_in(key, 41), -4.0, 4.0, (8, PROJ), jnp.float32)
    block_rows = directions[channel_blocks()]
    return ((entries + 0.6 * block_rows) * scales[None, :] / (5.0 * math.sqrt(FEATURE_DEPTH))).astype(jnp.bfloat16)


def draw_prototypes(key, part):
    key_entries = jax.random.fold_in(key, 31)
    raw_picks = jax.random.randint(jax.random.fold_in(key, 33), (PROTOS,), 0, 36)
    rotation = jax.random.randint(jax.random.fold_in(key, 34), (), 0, 8)
    member_group = (3 * class_of(raw_picks) + rotation) % 8
    shape = (PROJ, PROTOS)
    scales = embed_scales(key, 10.0)
    entries = jax.random.truncated_normal(key_entries, -4.0, 4.0, shape, jnp.float32)
    directions = jax.random.truncated_normal(jax.random.fold_in(key, 41), -4.0, 4.0, (8, PROJ), jnp.float32)
    strength = jax.random.uniform(jax.random.fold_in(key, 35), (PROTOS,), jnp.float32, 0.1, 0.7)
    member_dirs = jnp.transpose(directions[member_group])
    return ((entries + strength[None, :] * member_dirs) * scales[:, None]).astype(jnp.bfloat16)


def block_scale(rng, shape, pieces, low, largest):
    def one(dim, parts):
        draws = jax.random.uniform(jax.random.fold_in(jax.random.fold_in(rng, 6), dim), (parts,), jnp.float32, low / len(pieces), largest / len(pieces))
        return jnp.repeat(jnp.exp(draws), shape[dim] // parts).reshape((-1,) + (1,) * (len(shape) - dim - 1))

    level = one(*pieces[0])
    for cut in pieces[1:]:
        level = level * one(*cut)
    return level


def scatter_about(stream_key, shape, deviation, limit, split=(), held_as=jnp.bfloat16):
    result = deviation * jax.random.normal(stream_key, shape, jnp.float32)
    if split:
        result = result * block_scale(stream_key, shape, split, -0.22, 0.18)
    return jnp.clip(result, -limit, limit).astype(held_as)


def setup_inputs(seed: int = 0) -> dict:
    key_of = jax.random.split(jax.random.key(seed), 5)
    return {
        "features": draw_features(jax.random.fold_in(key_of[4], 71), 0),
        "conv_weight": scatter_about(key_of[1], (GROUPS, 9 * GW, GW), (9 * GW) ** -0.5, 0.09375, ((2, 8),)),
        "proj_weight": draw_proj_weight(jax.random.fold_in(key_of[4], 71), 0),
        "prototypes": draw_prototypes(jax.random.fold_in(key_of[4], 71), 0),
    }


logit_sharpening_divisor = 0.05
epsilon_norm = 1e-06

def conv_pool(images, kernel):
    img_count, side_len, _, group_count, group_width = images.shape
    padded = jnp.pad(images, ((0, 0), (1, 1), (1, 1), (0, 0), (0, 0))).astype(jnp.float32)
    kernel_wide = kernel.astype(jnp.float32)
    running = jnp.zeros(images.shape, jnp.float32)
    for tap_index in range(9):
        row_offset, col_shift = divmod(tap_index, 3)
        window = padded[:, row_offset:row_offset + side_len, col_shift:col_shift + side_len]
        tap_weights = kernel_wide[:, tap_index * group_width:(tap_index + 1) * group_width, :]
        running = running + jnp.einsum('bhwgi,gio->bhwgo', window, tap_weights)
    rectified_output = jax.nn.relu(running + images.astype(jnp.float32))
    return lax.optimization_barrier(jnp.mean(rectified_output, axis=(1, 2)))

def reference(features, conv_weight, proj_weight, prototypes):
    blocks = features.reshape((IMAGES // IMG_DEV, IMG_DEV) + features.shape[1:])
    pooled = lax.map(lambda block: conv_pool(block, conv_weight), blocks)
    pooled = pooled.reshape(IMAGES, GROUPS * GW)
    projected = jnp.dot(pooled.astype(jnp.bfloat16), proj_weight, preferred_element_type=jnp.float32)
    image_embedding = (projected / jnp.sqrt(lax.optimization_barrier(jnp.sum(projected * projected, axis=1, keepdims=True)) + epsilon_norm)).astype(jnp.bfloat16)
    protos_wide = prototypes.astype(jnp.float32)
    normalized_prototypes = (protos_wide / jnp.sqrt(lax.optimization_barrier(jnp.sum(protos_wide * protos_wide, axis=0, keepdims=True)) + epsilon_norm)).astype(jnp.bfloat16)
    cluster_similarity_logits = jnp.dot(image_embedding, normalized_prototypes, preferred_element_type=jnp.float32)
    probabilistic_cluster_share = jnp.exp(cluster_similarity_logits / logit_sharpening_divisor)
    for sweep in range(SINK):
        probabilistic_cluster_share = probabilistic_cluster_share / lax.optimization_barrier(jnp.sum(probabilistic_cluster_share, axis=0, keepdims=True))
        probabilistic_cluster_share = probabilistic_cluster_share / lax.optimization_barrier(jnp.sum(probabilistic_cluster_share, axis=1, keepdims=True))
    return PROTOS * probabilistic_cluster_share
```

```python
import jax
import jax.numpy as jnp
from jax import lax
from jax.experimental import pallas as pl
from jax.experimental.pallas import tpu as pltpu
from jax.sharding import PartitionSpec as P

MESH = pl.DeviceIdType.MESH
F32 = jnp.float32
BF16 = jnp.bfloat16

SINK = 3
PROTOS = 3072
EPS = 1e-06
TEMP = 0.05

N = 8
ROWS = 32
MAP = 14 * ROWS
KQ = 1152
HALF = PROTOS // 2
SLICE = 384


def device(x, y, z, c):
    dp = lax.rem(x, N) * 16 + (lax.rem(z, N) // 4) * 8 + lax.rem(y, N)
    return dp, lax.rem(z, 4) * 2 + lax.rem(c, 2)


def nt(a, b):
    return lax.dot_general(a, b, (((1,), (1,)), ((), ())), preferred_element_type=F32)


def split_rows(v):
    hi = v.astype(BF16).astype(F32)
    row = lax.broadcasted_iota(jnp.int32, (16, v.shape[1]), 0)
    return jnp.where(row == 0, hi, jnp.where(row == 1, v - hi, 0.0)).astype(BF16)


def kernel(
    x_hbm, w_hbm, proj_hbm, proto_hbm, out_ref,
    wide, sib, xf, xs, acc, gath, proj, proto, prs, part, zb, yb, ef, ehi, elo, cb, rb, fin,
    loc, sib_s, sib_r, p1_s, p1_r, p2_s, p2_r, pr_s, pr_r, pt_s, pt_r,
    d1_s, d1_r, d2_s, d2_r, c_s, c_r, r_s, r_r, f_s, f_r,
):
    dp, fs = lax.axis_index("dp"), lax.axis_index("fsdp")
    x, y, zh = dp // 16, lax.rem(dp, 8), lax.rem(dp // 8, 2)
    zl, c = fs // 2, lax.rem(fs, 2)
    z = zh * 4 + zl
    sibling = device(x, y, z, c + 1)
    zpeer = [None] + [device(x, y, z + k, c) for k in range(1, N)]
    ypeer = [None] + [device(x, y + k, z, c) for k in range(1, N)]
    xpeer = [None] + [device(x + k, y, z, c) for k in range(1, N)]

    def send(src, dst, s, r, to):
        pltpu.make_async_remote_copy(
            src_ref=src, dst_ref=dst, send_sem=s, recv_sem=r, device_id=to, device_id_type=MESH
        ).start()

    def wait(ref, sem):
        pltpu.make_async_copy(ref, ref, sem).wait()

    own = pl.ds(pl.multiple_of(zl * 64, 64), 64)
    for q in range(4):
        pltpu.make_async_copy(
            w_hbm.at[:, pl.ds(q * KQ, KQ)], gath.at[own, pl.ds(q * KQ, KQ)], loc.at[0]
        ).start()
    pltpu.make_async_copy(proto_hbm, proto, loc.at[1]).start()
    pltpu.make_async_copy(x_hbm, wide, loc.at[2]).start()
    pltpu.make_async_copy(proj_hbm, proj, loc.at[3]).start()

    barrier = pltpu.get_barrier_semaphore()
    for to in [sibling] + zpeer[1:] + ypeer[1:] + xpeer[1:]:
        pl.semaphore_signal(barrier, inc=1, device_id=to, device_id_type=MESH)

    pltpu.make_async_copy(proto_hbm, proto, loc.at[1]).wait()
    pw = proto[...].astype(F32)
    norm = jnp.sqrt(jnp.sum(pw * pw, axis=0, keepdims=True) + EPS)
    prs[zl] = (pw / norm).astype(BF16)
    pltpu.make_async_copy(x_hbm, wide, loc.at[2]).wait()
    wait(gath.at[pl.ds(0, 64), :], loc.at[0])

    pl.semaphore_wait(barrier, 1 + 3 * (N - 1))

    color = [lax.rem(x + 2 * y, 4), lax.rem(2 * x + y, 4)]

    def piece(s, h, g=None):
        row = s * 64 + h * 32
        rows = pl.ds(pl.multiple_of(row, 32), 32)
        if g is not None:
            rows = pl.ds(pl.multiple_of(row + 16 * g, 16), 16)
        return gath.at[rows, pl.ds(pl.multiple_of(color[h] * KQ, 128), KQ)]

    for h in range(2):
        mine = piece(zl, h)
        send(mine, mine, p1_s, p1_r.at[0, h], zpeer[7])
        send(mine, mine, p1_s, p1_r.at[2, h], zpeer[1])
    for h in range(2):
        for g, k in ((0, 2), (1, 6)):
            mine = piece(zl, h, g)
            send(mine, mine, p1_s, p1_r.at[1, h], zpeer[k])
    send(wide, sib, sib_s, sib_r, sibling)

    def spread(src, slot):
        xf[pl.ds(0, 48), :] = jnp.zeros((48, 512), F32)
        xf[pl.ds(48, MAP), :] = src[...].astype(F32)
        xf[pl.ds(48 + MAP, 48), :] = jnp.zeros((48, 512), F32)
        for j in range(3):
            xs[slot, j] = xf[pl.ds(14 + 2 * j, 512), :].astype(BF16)

    spread(wide, c)

    def forward(k, h):
        s = lax.rem(zl + k, 4)
        full, part_ = (xpeer, ypeer) if h == 0 else (ypeer, xpeer)
        wait(piece(s, h), p1_r.at[k - 1, h])
        for to in (full[1], full[7]):
            send(piece(s, h), piece(s, h), p2_s, p2_r, to)
        for g, to in ((0, part_[1]), (1, part_[7])):
            send(piece(s, h, g), piece(s, h, g), p2_s, p2_r, to)

    for k in (1, 3, 2):
        for h in range(2):
            forward(k, h)

    for to in (zpeer[1], zpeer[7]):
        send(prs.at[zl], prs.at[zl], pr_s, pr_r, to)
    for g, to in ((0, zpeer[2]), (1, zpeer[6])):
        rows = pl.ds(128 * g, 128)
        send(prs.at[zl, rows], prs.at[zl, rows], pr_s, pr_r, to)

    wait(sib, sib_r)
    spread(sib, 1 - c)

    o = lax.broadcasted_iota(jnp.int32, (256, 512), 0)
    i = lax.broadcasted_iota(jnp.int32, (256, 512), 1)
    pick = jnp.where(i == (o // 64) * 128 + 64 * c + lax.rem(o, 64), 1.0, 0.0).astype(BF16)
    for slot in range(2):
        acc[slot] = nt(xs[slot, 1, pl.ds(32, MAP), :], pick)

    wait(gath.at[pl.ds(0, 144), :], p2_r)

    def conv(slot, carry):
        for t in range(9):
            r, j = divmod(t, 3)
            acc[slot] += nt(xs[slot, j, pl.ds(32 * r, MAP), :], gath[:, pl.ds(512 * t, 512)])
        return carry

    lax.fori_loop(0, 2, conv, 0)

    row32 = lax.broadcasted_iota(jnp.int32, (ROWS, 256), 0)
    row16 = lax.broadcasted_iota(jnp.int32, (16, 256), 0)
    pooled = jnp.zeros((16, 256), F32)
    for slot in range(2):
        line = jnp.sum(jnp.maximum(acc[slot].reshape(14, ROWS, 256), 0.0), axis=0)
        for b in range(2):
            keep = (lax.rem(row32, 2) == b) & (row32 < 28)
            mean = jnp.sum(jnp.where(keep, line, 0.0), axis=0, keepdims=True) / 196.0
            pooled = jnp.where(lax.rem(row16, 4) == 2 * slot + b, mean, pooled)

    pltpu.make_async_copy(proj_hbm, proj, loc.at[3]).wait()
    weights = jnp.concatenate(
        [proj[pl.ds(pl.multiple_of(128 * a + 64 * c, 64), 64), :] for a in range(4)], axis=0
    )
    partial = jnp.dot(pooled.astype(BF16), weights, preferred_element_type=F32)
    part[0] = partial[:8]
    send(part.at[0], part.at[1], pt_s, pt_r, sibling)
    wait(part.at[1], pt_r)
    projected = part[0] + part[1]
    norm = jnp.sqrt(jnp.sum(projected * projected, axis=1, keepdims=True) + EPS)
    embed = (projected / norm).astype(BF16).astype(F32)

    row8 = lax.broadcasted_iota(jnp.int32, (8, 256), 0)
    zb[z] = jnp.where(row8 // 4 == lax.rem(z, 2), embed, 0.0)
    for k in range(1, N):
        send(zb.at[z], zb.at[z], d1_s, d1_r, zpeer[k])
    wait(zb.at[pl.ds(0, N - 1)], d1_r)
    yb[N - 1] = jnp.concatenate([zb[2 * k] + zb[2 * k + 1] for k in range(4)], axis=0).astype(BF16)
    for k in range(1, N):
        send(yb.at[N - 1], yb.at[k - 1], d2_s, d2_r, ypeer[k])
    wait(prs.at[pl.ds(0, 3)], pr_r)
    wait(yb.at[pl.ds(0, N - 1)], d2_r)

    images = yb[...].reshape(256, 256)
    for a in range(4):
        cols = pl.ds(SLICE * a, SLICE)
        e = jnp.exp(jnp.dot(images, prs[a], preferred_element_type=F32) / TEMP)
        ef[:, cols] = e
        hi = e.astype(BF16)
        ehi[:, cols] = hi
        elo[:, cols] = (e - hi.astype(F32)).astype(BF16)
        cb[0, N - 1, :, cols] = jnp.sum(e, axis=0, keepdims=True)

    for sweep in range(SINK):
        for k in range(1, N):
            send(cb.at[sweep, N - 1], cb.at[sweep, k - 1], c_s.at[sweep], c_r.at[sweep], xpeer[k])
        wait(cb.at[sweep, pl.ds(0, N - 1)], c_r.at[sweep])
        total = cb[sweep, 0]
        for k in range(1, N):
            total = total + cb[sweep, k]
        v = 1.0 / total
        if sweep == SINK - 1:
            break
        vv = split_rows(v)
        s = nt(vv, ehi[...]) + nt(vv, elo[...])
        rb[sweep, 0] = s[0:1] + s[1:2]
        send(rb.at[sweep, 0], rb.at[sweep, 1], r_s.at[sweep], r_r.at[sweep], sibling)
        wait(rb.at[sweep, 1], r_r.at[sweep])
        uu = split_rows(1.0 / (rb[sweep, 0] + rb[sweep, 1]))
        s = jnp.dot(uu, ehi[...], preferred_element_type=F32)
        s = s + jnp.dot(uu, elo[...], preferred_element_type=F32)
        cb[sweep + 1, N - 1] = s[0:1] + s[1:2]

    block = pl.ds(pl.multiple_of(32 * (N - 1) + 8 * (z // 2), 8), 8)
    fin[0] = ef[block, :] * v
    send(fin.at[0], fin.at[1], f_s, f_r, sibling)
    wait(fin.at[1], f_r)
    even = jnp.where(c == 0, fin[0], fin[1])
    odd = jnp.where(c == 0, fin[1], fin[0])
    rows = jnp.sum(even, axis=1, keepdims=True) + jnp.sum(odd, axis=1, keepdims=True)
    scale = PROTOS / rows
    even, odd = even * scale, odd * scale
    first = lax.rem(z, 2) * 4 + 2 * c
    rowc = lax.broadcasted_iota(jnp.int32, (8, SLICE), 0)
    for b in range(2):
        for a in range(4):
            for half, codes in ((0, even), (1, odd)):
                mine = jnp.where(rowc == first + b, codes[:, SLICE * a : SLICE * (a + 1)], 0.0)
                out_ref[pl.ds(b, 1), pl.ds(SLICE * (2 * a + half), SLICE)] = jnp.sum(
                    mine, axis=0, keepdims=True
                )

    wait(gath.at[pl.ds(0, 48), :], p1_s)
    wait(gath.at[pl.ds(0, 144), :], p2_s)
    wait(wide, sib_s)
    wait(prs.at[pl.ds(0, 3)], pr_s)
    wait(part.at[0], pt_s)
    wait(zb.at[pl.ds(0, N - 1)], d1_s)
    wait(yb.at[pl.ds(0, N - 1)], d2_s)
    for sweep in range(SINK):
        wait(cb.at[sweep, pl.ds(0, N - 1)], c_s.at[sweep])
    for sweep in range(SINK - 1):
        wait(rb.at[sweep, 0], r_s.at[sweep])
    wait(fin.at[0], f_s)


def shards(features, conv_weight, proj_weight, prototypes):
    maps = jnp.transpose(features[:, :, :, 0, :], (1, 2, 0, 3))
    maps = jnp.pad(maps, ((0, 0), (0, 2), (0, 0), (0, 0))).reshape(MAP, 512)
    weight = jnp.transpose(conv_weight[0])
    dma = pltpu.SemaphoreType.DMA
    return pl.pallas_call(
        kernel,
        out_shape=jax.ShapeDtypeStruct((2, PROTOS), F32),
        in_specs=[pl.BlockSpec(memory_space=pl.ANY)] * 4,
        out_specs=pl.BlockSpec(memory_space=pltpu.VMEM),
        scratch_shapes=[
            pltpu.VMEM((MAP, 512), BF16),
            pltpu.VMEM((MAP, 512), BF16),
            pltpu.VMEM((MAP + 96, 512), F32),
            pltpu.VMEM((2, 3, 512, 512), BF16),
            pltpu.VMEM((2, MAP, 256), F32),
            pltpu.VMEM((256, 4 * KQ), BF16),
            pltpu.VMEM((512, 256), BF16),
            pltpu.VMEM((256, SLICE), BF16),
            pltpu.VMEM((4, 256, SLICE), BF16),
            pltpu.VMEM((2, 8, 256), F32),
            pltpu.VMEM((N, 8, 256), F32),
            pltpu.VMEM((N, 32, 256), BF16),
            pltpu.VMEM((256, HALF), F32),
            pltpu.VMEM((256, HALF), BF16),
            pltpu.VMEM((256, HALF), BF16),
            pltpu.VMEM((SINK, N, 1, HALF), F32),
            pltpu.VMEM((SINK - 1, 2, 1, 256), F32),
            pltpu.VMEM((2, 8, HALF), F32),
            dma((4,)),
            dma, dma,
            dma, dma((3, 2)),
            dma, dma,
            dma, dma,
            dma, dma,
            dma, dma,
            dma, dma,
            dma((SINK,)), dma((SINK,)),
            dma((SINK - 1,)), dma((SINK - 1,)),
            dma, dma,
        ],
        compiler_params=pltpu.CompilerParams(
            collective_id=0, has_side_effects=True, vmem_limit_bytes=48 * 1024 * 1024
        ),
    )(maps, weight, proj_weight, prototypes)


def solution(mesh):
    return jax.shard_map(
        shards,
        mesh=mesh,
        in_specs=(
            P(("dp", "fsdp"), None, None, None, None),
            P(None, None, "fsdp"),
            P(),
            P(None, "fsdp"),
        ),
        out_specs=P(("dp", "fsdp"), None),
        check_vma=False,
    )
```

```python
import jax
import jax.numpy as jnp
from jax import lax
from jax.experimental import pallas as pl
from jax.experimental.pallas import tpu as pltpu
from jax.sharding import PartitionSpec as P

MESH = pl.DeviceIdType.MESH
F32 = jnp.float32
BF16 = jnp.bfloat16

SINK = 3
PROTOS = 3072
EPS = 1e-06
TEMP = 0.05

N = 8
ROWS = 32
MAP = 14 * ROWS
KQ = 1152
HALF = PROTOS // 2
SLICE = 384


def device(x, y, z, c):
    dp = lax.rem(x, N) * 16 + (lax.rem(z, N) // 4) * 8 + lax.rem(y, N)
    return dp, lax.rem(z, 4) * 2 + lax.rem(c, 2)


def nt(a, b):
    return lax.dot_general(a, b, (((1,), (1,)), ((), ())), preferred_element_type=F32)


def split_rows(v):
    hi = v.astype(BF16).astype(F32)
    row = lax.broadcasted_iota(jnp.int32, (16, v.shape[1]), 0)
    return jnp.where(row == 0, hi, jnp.where(row == 1, v - hi, 0.0)).astype(BF16)


def kernel(
    x_hbm, w_hbm, proj_hbm, proto_hbm, out_ref,
    wide, sib, xf, xs, acc, gath, proj, proto, prs, part, zb, yb, ef, eh, cb, rb, fin,
    loc, sib_s, sib_r, p1_s, p1_r, p2_s, p2_r, pr_s, pr_r, pt_s, pt_r,
    d1_s, d1_r, d2_s, d2_r, c_s, c_r, r_s, r_r, f_s, f_r, far,
):
    dp, fs = lax.axis_index("dp"), lax.axis_index("fsdp")
    x, y, zh = dp // 16, lax.rem(dp, 8), lax.rem(dp // 8, 2)
    zl, c = fs // 2, lax.rem(fs, 2)
    z = zh * 4 + zl
    sibling = device(x, y, z, c + 1)
    zpeer = [None] + [device(x, y, z + k, c) for k in range(1, N)]
    ypeer = [None] + [device(x, y + k, z, c) for k in range(1, N)]
    xpeer = [None] + [device(x + k, y, z, c) for k in range(1, N)]

    def send(src, dst, s, r, to):
        pltpu.make_async_remote_copy(
            src_ref=src, dst_ref=dst, send_sem=s, recv_sem=r, device_id=to, device_id_type=MESH
        ).start()

    def wait(ref, sem):
        pltpu.make_async_copy(ref, ref, sem).wait()

    due = []

    def drain():
        for ref, sem in due + late:
            wait(ref, sem)

    own = pl.ds(pl.multiple_of(zl * 64, 64), 64)
    for q in range(4):
        pltpu.make_async_copy(
            w_hbm.at[:, pl.ds(q * KQ, KQ)], gath.at[own, pl.ds(q * KQ, KQ)], loc.at[0]
        ).start()
    pltpu.make_async_copy(proto_hbm, proto, loc.at[1]).start()
    pltpu.make_async_copy(x_hbm, wide, loc.at[2]).start()
    pltpu.make_async_copy(proj_hbm, proj, loc.at[3]).start()

    late = []
    barrier = pltpu.get_barrier_semaphore()
    near = [p[k] for p in (zpeer, xpeer, ypeer) for k in (1, 7, 2, 6)]
    for to in [sibling] + near:
        pl.semaphore_signal(barrier, inc=1, device_id=to, device_id_type=MESH)

    pltpu.make_async_copy(proto_hbm, proto, loc.at[1]).wait()
    pw = proto[...].astype(F32)
    norm = jnp.sqrt(jnp.sum(pw * pw, axis=0, keepdims=True) + EPS)
    prs[zl] = (pw / norm).astype(BF16)

    def spread(src, slot):
        xf[...] = jnp.zeros((MAP + 96, 512), F32)
        for h in range(14):
            xf[pl.ds(48 + ROWS * h, 28), :] = src[h].astype(F32).reshape(28, 512)
        for j in range(3):
            xs[slot, j] = xf[pl.ds(14 + 2 * j, 512), :].astype(BF16)

    pltpu.make_async_copy(x_hbm, wide, loc.at[2]).wait()
    spread(wide, c)
    wait(gath.at[pl.ds(0, 64), :], loc.at[0])
    pltpu.make_async_copy(proj_hbm, proj, loc.at[3]).wait()

    pl.semaphore_wait(barrier, 1 + len(near))

    color = [lax.rem(x + 2 * y, 4), lax.rem(2 * x + y, 4)]

    def piece(s, h, g=None):
        row = s * 64 + h * 32
        rows = pl.ds(pl.multiple_of(row, 32), 32)
        if g is not None:
            rows = pl.ds(pl.multiple_of(row + 16 * g, 16), 16)
        return gath.at[rows, pl.ds(pl.multiple_of(color[h] * KQ, 128), KQ)]

    for h in range(2):
        mine = piece(zl, h)
        send(mine, mine, p1_s, p1_r.at[0, h], zpeer[7])
        send(mine, mine, p1_s, p1_r.at[2, h], zpeer[1])
    for h in range(2):
        for g, k in ((0, 2), (1, 6)):
            mine = piece(zl, h, g)
            send(mine, mine, p1_s, p1_r.at[1, h], zpeer[k])
    send(wide, sib, sib_s, sib_r, sibling)
    due.append((gath.at[pl.ds(0, 48), :], p1_s))
    due.append((wide, sib_s))
    late = [(sib, sib_r)]
    for to in [p[k] for p in (zpeer, xpeer, ypeer) for k in (2, 6)]:
        pl.semaphore_signal(far, inc=1, device_id=to, device_id_type=MESH)

    def forward(k, h):
        s = lax.rem(zl + k, 4)
        full, part_ = (xpeer, ypeer) if h == 0 else (ypeer, xpeer)
        wait(piece(s, h), p1_r.at[k - 1, h])
        for to in (full[1], full[7]):
            send(piece(s, h), piece(s, h), p2_s, p2_r, to)
        for g, to in ((0, part_[1]), (1, part_[7])):
            send(piece(s, h, g), piece(s, h, g), p2_s, p2_r, to)

    for k, h in ((1, 0), (3, 0), (1, 1), (3, 1), (2, 0), (2, 1)):
        forward(k, h)

    due.append((gath.at[pl.ds(0, 144), :], p2_s))
    late.append((gath.at[pl.ds(0, 144), :], p2_r))
    for to in (zpeer[1], zpeer[7]):
        send(prs.at[zl], prs.at[zl], pr_s, pr_r, to)
    for g, to in ((0, zpeer[2]), (1, zpeer[6])):
        rows = pl.ds(128 * g, 128)
        send(prs.at[zl, rows], prs.at[zl, rows], pr_s, pr_r, to)

    due.append((prs.at[pl.ds(0, 3)], pr_s))
    late.append((prs.at[pl.ds(0, 3)], pr_r))
    pl.semaphore_wait(far, 6)
    wait(*late.pop(0))
    spread(sib, 1 - c)

    o = lax.broadcasted_iota(jnp.int32, (256, 512), 0)
    i = lax.broadcasted_iota(jnp.int32, (256, 512), 1)
    pick = jnp.where(i == (o // 64) * 128 + 64 * c + lax.rem(o, 64), 1.0, 0.0).astype(BF16)
    for slot in range(2):
        acc[slot] = nt(xs[slot, 1, pl.ds(32, MAP), :], pick)

    wait(*late.pop(0))

    def conv(slot, carry):
        for t in range(9):
            r, j = divmod(t, 3)
            acc[slot] += nt(xs[slot, j, pl.ds(32 * r, MAP), :], gath[:, pl.ds(512 * t, 512)])
        return carry

    lax.fori_loop(0, 2, conv, 0)

    row32 = lax.broadcasted_iota(jnp.int32, (ROWS, 256), 0)
    row16 = lax.broadcasted_iota(jnp.int32, (16, 256), 0)
    pooled = jnp.zeros((16, 256), F32)
    for slot in range(2):
        line = jnp.sum(jnp.maximum(acc[slot].reshape(14, ROWS, 256), 0.0), axis=0)
        for b in range(2):
            keep = (lax.rem(row32, 2) == b) & (row32 < 28)
            mean = jnp.sum(jnp.where(keep, line, 0.0), axis=0, keepdims=True) / 196.0
            pooled = jnp.where(lax.rem(row16, 4) == 2 * slot + b, mean, pooled)

    weights = jnp.concatenate(
        [proj[pl.ds(pl.multiple_of(128 * a + 64 * c, 64), 64), :] for a in range(4)], axis=0
    )
    partial = jnp.dot(pooled.astype(BF16), weights, preferred_element_type=F32)
    part[0] = partial[:8]
    send(part.at[0], part.at[1], pt_s, pt_r, sibling)
    due.append((part.at[0], pt_s))
    wait(part.at[1], pt_r)
    projected = part[0] + part[1]
    norm = jnp.sqrt(jnp.sum(projected * projected, axis=1, keepdims=True) + EPS)
    embed = (projected / norm).astype(BF16).astype(F32)

    row8 = lax.broadcasted_iota(jnp.int32, (8, 256), 0)
    zb[z] = jnp.where(row8 // 4 == lax.rem(z, 2), embed, 0.0).astype(BF16)
    for k in range(1, N):
        send(zb.at[z], zb.at[z], d1_s, d1_r, zpeer[k])
    due.append((zb.at[pl.ds(0, N - 1)], d1_s))
    wait(zb.at[pl.ds(0, N - 1)], d1_r)
    pairs = [zb[2 * k].astype(F32) + zb[2 * k + 1].astype(F32) for k in range(4)]
    yb[N - 1] = jnp.concatenate(pairs, axis=0).astype(BF16)
    for k in range(1, N):
        send(yb.at[N - 1], yb.at[k - 1], d2_s, d2_r, ypeer[k])
    due.append((yb.at[pl.ds(0, N - 1)], d2_s))
    wait(*late.pop(0))
    wait(yb.at[pl.ds(0, N - 1)], d2_r)

    images = yb[...].reshape(256, 256)
    for a in range(4):
        cols = pl.ds(SLICE * a, SLICE)
        e = jnp.exp(jnp.dot(images, prs[a], preferred_element_type=F32) / TEMP)
        ef[:, cols] = e
        eh[:, cols] = e.astype(BF16)
        cb[0, N - 1, :, cols] = jnp.sum(e, axis=0, keepdims=True)

    for sweep in range(SINK):
        for k in range(1, N):
            send(cb.at[sweep, N - 1], cb.at[sweep, k - 1], c_s.at[sweep], c_r.at[sweep], xpeer[k])
        due.append((cb.at[sweep, pl.ds(0, N - 1)], c_s.at[sweep]))
        wait(cb.at[sweep, pl.ds(0, N - 1)], c_r.at[sweep])
        total = cb[sweep, 0]
        for k in range(1, N):
            total = total + cb[sweep, k]
        v = 1.0 / total
        if sweep == SINK - 1:
            break
        vv = split_rows(v)
        s = nt(vv, eh[...])
        rb[sweep, 0] = s[0:1] + s[1:2]
        send(rb.at[sweep, 0], rb.at[sweep, 1], r_s.at[sweep], r_r.at[sweep], sibling)
        due.append((rb.at[sweep, 0], r_s.at[sweep]))
        wait(rb.at[sweep, 1], r_r.at[sweep])
        uu = split_rows(1.0 / (rb[sweep, 0] + rb[sweep, 1]))
        s = jnp.dot(uu, eh[...], preferred_element_type=F32)
        cb[sweep + 1, N - 1] = s[0:1] + s[1:2]

    block = pl.ds(pl.multiple_of(32 * (N - 1) + 8 * (z // 2), 8), 8)
    fin[0] = ef[block, :] * v
    send(fin.at[0], fin.at[1], f_s, f_r, sibling)
    due.append((fin.at[0], f_s))
    wait(fin.at[1], f_r)
    even = jnp.where(c == 0, fin[0], fin[1])
    odd = jnp.where(c == 0, fin[1], fin[0])
    rows = jnp.sum(even, axis=1, keepdims=True) + jnp.sum(odd, axis=1, keepdims=True)
    scale = PROTOS / rows
    even, odd = even * scale, odd * scale
    first = lax.rem(z, 2) * 4 + 2 * c
    rowc = lax.broadcasted_iota(jnp.int32, (8, SLICE), 0)
    for b in range(2):
        for a in range(4):
            for half, codes in ((0, even), (1, odd)):
                mine = jnp.where(rowc == first + b, codes[:, SLICE * a : SLICE * (a + 1)], 0.0)
                out_ref[pl.ds(b, 1), pl.ds(SLICE * (2 * a + half), SLICE)] = jnp.sum(
                    mine, axis=0, keepdims=True
                )

    drain()


def shards(features, conv_weight, proj_weight, prototypes):
    maps = jnp.transpose(features[:, :, :, 0, :], (1, 2, 0, 3))
    weight = jnp.transpose(conv_weight[0])
    dma = pltpu.SemaphoreType.DMA
    return pl.pallas_call(
        kernel,
        out_shape=jax.ShapeDtypeStruct((2, PROTOS), F32),
        in_specs=[pl.BlockSpec(memory_space=pltpu.HBM)] * 4,
        out_specs=pl.BlockSpec(memory_space=pltpu.VMEM),
        scratch_shapes=[
            pltpu.VMEM((14, 14, 2, 512), BF16),
            pltpu.VMEM((14, 14, 2, 512), BF16),
            pltpu.VMEM((MAP + 96, 512), F32),
            pltpu.VMEM((2, 3, 512, 512), BF16),
            pltpu.VMEM((2, MAP, 256), F32),
            pltpu.VMEM((256, 4 * KQ), BF16),
            pltpu.VMEM((512, 256), BF16),
            pltpu.VMEM((256, SLICE), BF16),
            pltpu.VMEM((4, 256, SLICE), BF16),
            pltpu.VMEM((2, 8, 256), F32),
            pltpu.VMEM((N, 8, 256), BF16),
            pltpu.VMEM((N, 32, 256), BF16),
            pltpu.VMEM((256, HALF), F32),
            pltpu.VMEM((256, HALF), BF16),
            pltpu.VMEM((SINK, N, 1, HALF), F32),
            pltpu.VMEM((SINK - 1, 2, 1, 256), F32),
            pltpu.VMEM((2, 8, HALF), F32),
            dma((4,)),
            dma, dma,
            dma, dma((3, 2)),
            dma, dma,
            dma, dma,
            dma, dma,
            dma, dma,
            dma, dma,
            dma((SINK,)), dma((SINK,)),
            dma((SINK - 1,)), dma((SINK - 1,)),
            dma, dma,
            pltpu.SemaphoreType.REGULAR,
        ],
        compiler_params=pltpu.CompilerParams(
            collective_id=0, has_side_effects=True, vmem_limit_bytes=48000 * 1024
        ),
    )(*[pltpu.with_memory_space_constraint(a, pltpu.HBM) for a in (maps, weight, proj_weight, prototypes)])


def solution(mesh):
    return jax.shard_map(
        shards,
        mesh=mesh,
        in_specs=(
            P(("dp", "fsdp"), None, None, None, None),
            P(None, None, "fsdp"),
            P(),
            P(None, "fsdp"),
        ),
        out_specs=P(("dp", "fsdp"), None),
        check_vma=False,
    )
```

```python
import jax
import jax.numpy as jnp
from jax import lax
from jax.experimental import pallas as pl
from jax.experimental.pallas import tpu as pltpu
from jax.sharding import PartitionSpec as P

MESH = pl.DeviceIdType.MESH
F32 = jnp.float32
BF16 = jnp.bfloat16

SINK = 3
PROTOS = 3072
EPS = 1e-06
TEMP = 0.05

N = 8
ROWS = 32
MAP = 14 * ROWS
STAGES = ((0, 640), (2560, 512))
HALF = PROTOS // 2
SLICE = 384


def device(x, y, z, c):
    dp = lax.rem(x, N) * 16 + (lax.rem(z, N) // 4) * 8 + lax.rem(y, N)
    return dp, lax.rem(z, 4) * 2 + lax.rem(c, 2)


def nt(a, b):
    return lax.dot_general(a, b, (((1,), (1,)), ((), ())), preferred_element_type=F32)


def split_rows(v):
    hi = v.astype(BF16).astype(F32)
    row = lax.broadcasted_iota(jnp.int32, (16, v.shape[1]), 0)
    return jnp.where(row == 0, hi, jnp.where(row == 1, v - hi, 0.0)).astype(BF16)


def kernel(
    x_hbm, w_hbm, proj_hbm, proto_hbm, out_ref,
    wide, sib, xf, xs, acc, gath, proj, proto, prs, part, zb, yb, ef, eh, cb, rb, fin,
    loc, sib_s, sib_r, p1_s, p1_r, p2_s, p2_r, pr_s, pr_r, pt_s, pt_r,
    d1_s, d1_r, d2_s, d2_r, c_s, c_r, r_s, r_r, f_s, f_r, far,
):
    dp, fs = lax.axis_index("dp"), lax.axis_index("fsdp")
    x, y, zh = dp // 16, lax.rem(dp, 8), lax.rem(dp // 8, 2)
    zl, c = fs // 2, lax.rem(fs, 2)
    z = zh * 4 + zl
    sibling = device(x, y, z, c + 1)
    zpeer = [None] + [device(x, y, z + k, c) for k in range(1, N)]
    ypeer = [None] + [device(x, y + k, z, c) for k in range(1, N)]
    xpeer = [None] + [device(x + k, y, z, c) for k in range(1, N)]

    def send(src, dst, s, r, to):
        pltpu.make_async_remote_copy(
            src_ref=src, dst_ref=dst, send_sem=s, recv_sem=r, device_id=to, device_id_type=MESH
        ).start()

    def wait(ref, sem):
        pltpu.make_async_copy(ref, ref, sem).wait()

    due = []

    def drain():
        for ref, sem in due + late:
            wait(ref, sem)

    late = []
    barrier = pltpu.get_barrier_semaphore()
    near = [p[k] for p in (zpeer, xpeer, ypeer) for k in (1, 7, 2, 6)]
    for to in [sibling] + near:
        pl.semaphore_signal(barrier, inc=1, device_id=to, device_id_type=MESH)

    own = pl.ds(pl.multiple_of(zl * 64, 64), 64)
    pltpu.make_async_copy(w_hbm, gath.at[own], loc.at[0]).start()
    pltpu.make_async_copy(proto_hbm, proto, loc.at[1]).start()
    pltpu.make_async_copy(x_hbm, wide, loc.at[2]).start()
    pltpu.make_async_copy(proj_hbm, proj, loc.at[3]).start()

    pltpu.make_async_copy(proto_hbm, proto, loc.at[1]).wait()
    pw = proto[...].astype(F32)
    norm = jnp.sqrt(jnp.sum(pw * pw, axis=0, keepdims=True) + EPS)
    prs[zl] = (pw / norm).astype(BF16)

    def spread(src, slot):
        xf[...] = jnp.zeros((MAP + 96, 512), F32)
        for h in range(14):
            xf[pl.ds(48 + ROWS * h, 28), :] = src[h].astype(F32).reshape(28, 512)
        for j in range(3):
            xs[slot, j] = xf[pl.ds(14 + 2 * j, 512), :].astype(BF16)

    pltpu.make_async_copy(x_hbm, wide, loc.at[2]).wait()
    wait(gath.at[pl.ds(0, 64), :], loc.at[0])
    pltpu.make_async_copy(proj_hbm, proj, loc.at[3]).wait()

    pl.semaphore_wait(barrier, 1 + len(near))

    color = [lax.rem(x + 2 * y, 4), lax.rem(2 * x + y, 4)]

    def piece(stage, s, h, g=None):
        first, size = STAGES[stage]
        row = s * 64 + h * 32
        rows = pl.ds(pl.multiple_of(row, 32), 32)
        if g is not None:
            rows = pl.ds(pl.multiple_of(row + 16 * g, 16), 16)
        return gath.at[rows, pl.ds(pl.multiple_of(first + color[h] * size, 128), size)]

    for stage in range(2):
        for h in range(2):
            mine = piece(stage, zl, h)
            send(mine, mine, p1_s, p1_r.at[stage, 0, h], zpeer[7])
            send(mine, mine, p1_s, p1_r.at[stage, 2, h], zpeer[1])
        for h in range(2):
            for g, k in ((0, 2), (1, 6)):
                mine = piece(stage, zl, h, g)
                send(mine, mine, p1_s, p1_r.at[stage, 1, h], zpeer[k])
    send(wide, sib, sib_s, sib_r, sibling)
    due.append((gath.at[pl.ds(0, 48), :], p1_s))
    due.append((wide, sib_s))
    late = [(sib, sib_r)]
    for to in [p[k] for p in (zpeer, xpeer, ypeer) for k in (2, 6)]:
        pl.semaphore_signal(far, inc=1, device_id=to, device_id_type=MESH)

    spread(wide, c)

    def forward(stage, k, h):
        s = lax.rem(zl + k, 4)
        full, half = (xpeer, ypeer) if h == 0 else (ypeer, xpeer)
        whole = piece(stage, s, h)
        wait(whole, p1_r.at[stage, k - 1, h])
        for to in (full[1], full[7]):
            send(whole, whole, p2_s, p2_r.at[stage], to)
        for g, to in ((0, half[1]), (1, half[7])):
            mine = piece(stage, s, h, g)
            send(mine, mine, p2_s, p2_r.at[stage], to)

    for stage in range(2):
        for k, h in ((1, 0), (3, 0), (1, 1), (3, 1), (2, 0), (2, 1)):
            forward(stage, k, h)
    due.append((gath.at[pl.ds(0, 144), :], p2_s))
    late.append((gath.at[pl.ds(0, 80), :], p2_r.at[0]))
    late.append((gath.at[pl.ds(0, 64), :], p2_r.at[1]))
    for to in (zpeer[1], zpeer[7]):
        send(prs.at[zl], prs.at[zl], pr_s, pr_r, to)
    for g, to in ((0, zpeer[2]), (1, zpeer[6])):
        rows = pl.ds(128 * g, 128)
        send(prs.at[zl, rows], prs.at[zl, rows], pr_s, pr_r, to)

    due.append((prs.at[pl.ds(0, 3)], pr_s))
    late.append((prs.at[pl.ds(0, 3)], pr_r))
    pl.semaphore_wait(far, 6)
    wait(*late.pop(0))
    spread(sib, 1 - c)

    o = lax.broadcasted_iota(jnp.int32, (256, 512), 0)
    i = lax.broadcasted_iota(jnp.int32, (256, 512), 1)
    pick = jnp.where(i == (o // 64) * 128 + 64 * c + lax.rem(o, 64), 1.0, 0.0).astype(BF16)
    for slot in range(2):
        acc[slot] = nt(xs[slot, 1, pl.ds(32, MAP), :], pick)

    def conv(taps):
        def maps(slot, carry):
            for t in taps:
                r, j = divmod(t, 3)
                acc[slot] += nt(xs[slot, j, pl.ds(32 * r, MAP), :], gath[:, pl.ds(512 * t, 512)])
            return carry

        lax.fori_loop(0, 2, maps, 0)

    wait(*late.pop(0))
    conv(range(5))
    wait(*late.pop(0))
    conv(range(5, 9))

    row32 = lax.broadcasted_iota(jnp.int32, (ROWS, 256), 0)
    row16 = lax.broadcasted_iota(jnp.int32, (16, 256), 0)
    pooled = jnp.zeros((16, 256), F32)
    for slot in range(2):
        line = jnp.sum(jnp.maximum(acc[slot].reshape(14, ROWS, 256), 0.0), axis=0)
        for b in range(2):
            keep = (lax.rem(row32, 2) == b) & (row32 < 28)
            mean = jnp.sum(jnp.where(keep, line, 0.0), axis=0, keepdims=True) / 196.0
            pooled = jnp.where(lax.rem(row16, 4) == 2 * slot + b, mean, pooled)

    weights = jnp.concatenate(
        [proj[pl.ds(pl.multiple_of(128 * a + 64 * c, 64), 64), :] for a in range(4)], axis=0
    )
    partial = jnp.dot(pooled.astype(BF16), weights, preferred_element_type=F32)
    part[0] = partial[:8]
    send(part.at[0], part.at[1], pt_s, pt_r, sibling)
    due.append((part.at[0], pt_s))
    wait(part.at[1], pt_r)
    projected = part[0] + part[1]
    norm = jnp.sqrt(jnp.sum(projected * projected, axis=1, keepdims=True) + EPS)
    embed = (projected / norm).astype(BF16).astype(F32)

    row8 = lax.broadcasted_iota(jnp.int32, (8, 256), 0)
    zb[y] = jnp.where(row8 // 4 == lax.rem(y, 2), embed, 0.0).astype(BF16)
    for k in range(1, N):
        send(zb.at[y], zb.at[y], d1_s, d1_r, ypeer[k])
    due.append((zb.at[pl.ds(0, N - 1)], d1_s))
    wait(zb.at[pl.ds(0, N - 1)], d1_r)
    pairs = [zb[2 * k].astype(F32) + zb[2 * k + 1].astype(F32) for k in range(4)]
    yb[N - 1] = jnp.concatenate(pairs, axis=0).astype(BF16)
    for k in range(1, N):
        send(yb.at[N - 1], yb.at[k - 1], d2_s, d2_r, zpeer[k])
    due.append((yb.at[pl.ds(0, N - 1)], d2_s))
    wait(*late.pop(0))
    wait(yb.at[pl.ds(0, N - 1)], d2_r)

    images = yb[...].reshape(256, 256)
    for a in range(4):
        cols = pl.ds(SLICE * a, SLICE)
        e = jnp.exp(jnp.dot(images, prs[a], preferred_element_type=F32) / TEMP)
        ef[:, cols] = e
        eh[:, cols] = e.astype(BF16)
        cb[0, N - 1, :, cols] = jnp.sum(e, axis=0, keepdims=True)

    for sweep in range(SINK):
        for k in range(1, N):
            send(cb.at[sweep, N - 1], cb.at[sweep, k - 1], c_s.at[sweep], c_r.at[sweep], xpeer[k])
        due.append((cb.at[sweep, pl.ds(0, N - 1)], c_s.at[sweep]))
        wait(cb.at[sweep, pl.ds(0, N - 1)], c_r.at[sweep])
        total = cb[sweep, 0]
        for k in range(1, N):
            total = total + cb[sweep, k]
        v = 1.0 / total
        if sweep == SINK - 1:
            break
        vv = split_rows(v)
        s = nt(vv, eh[...])
        rb[sweep, 0] = s[0:1] + s[1:2]
        send(rb.at[sweep, 0], rb.at[sweep, 1], r_s.at[sweep], r_r.at[sweep], sibling)
        due.append((rb.at[sweep, 0], r_s.at[sweep]))
        wait(rb.at[sweep, 1], r_r.at[sweep])
        uu = split_rows(1.0 / (rb[sweep, 0] + rb[sweep, 1]))
        s = jnp.dot(uu, eh[...], preferred_element_type=F32)
        cb[sweep + 1, N - 1] = s[0:1] + s[1:2]

    block = pl.ds(pl.multiple_of(32 * (N - 1) + 8 * (y // 2), 8), 8)
    fin[0] = ef[block, :] * v
    send(fin.at[0], fin.at[1], f_s, f_r, sibling)
    due.append((fin.at[0], f_s))
    wait(fin.at[1], f_r)
    even = jnp.where(c == 0, fin[0], fin[1])
    odd = jnp.where(c == 0, fin[1], fin[0])
    rows = jnp.sum(even, axis=1, keepdims=True) + jnp.sum(odd, axis=1, keepdims=True)
    scale = PROTOS / rows
    even, odd = even * scale, odd * scale
    first = lax.rem(y, 2) * 4 + 2 * c
    rowc = lax.broadcasted_iota(jnp.int32, (8, SLICE), 0)
    for b in range(2):
        for a in range(4):
            for half, codes in ((0, even), (1, odd)):
                mine = jnp.where(rowc == first + b, codes[:, SLICE * a : SLICE * (a + 1)], 0.0)
                out_ref[pl.ds(b, 1), pl.ds(SLICE * (2 * a + half), SLICE)] = jnp.sum(
                    mine, axis=0, keepdims=True
                )

    drain()


def shards(features, conv_weight, proj_weight, prototypes):
    maps = jnp.transpose(features[:, :, :, 0, :], (1, 2, 0, 3))
    weight = jnp.transpose(conv_weight[0])
    dma = pltpu.SemaphoreType.DMA
    return pl.pallas_call(
        kernel,
        out_shape=jax.ShapeDtypeStruct((2, PROTOS), F32),
        in_specs=[pl.BlockSpec(memory_space=pltpu.HBM)] * 4,
        out_specs=pl.BlockSpec(memory_space=pltpu.VMEM),
        scratch_shapes=[
            pltpu.VMEM((14, 14, 2, 512), BF16),
            pltpu.VMEM((14, 14, 2, 512), BF16),
            pltpu.VMEM((MAP + 96, 512), F32),
            pltpu.VMEM((2, 3, 512, 512), BF16),
            pltpu.VMEM((2, MAP, 256), F32),
            pltpu.VMEM((256, 4608), BF16),
            pltpu.VMEM((512, 256), BF16),
            pltpu.VMEM((256, SLICE), BF16),
            pltpu.VMEM((4, 256, SLICE), BF16),
            pltpu.VMEM((2, 8, 256), F32),
            pltpu.VMEM((N, 8, 256), BF16),
            pltpu.VMEM((N, 32, 256), BF16),
            pltpu.VMEM((256, HALF), F32),
            pltpu.VMEM((256, HALF), BF16),
            pltpu.VMEM((SINK, N, 1, HALF), F32),
            pltpu.VMEM((SINK - 1, 2, 1, 256), F32),
            pltpu.VMEM((2, 8, HALF), F32),
            dma((4,)),
            dma, dma,
            dma, dma((2, 3, 2)),
            dma, dma((2,)),
            dma, dma,
            dma, dma,
            dma, dma,
            dma, dma,
            dma((SINK,)), dma((SINK,)),
            dma((SINK - 1,)), dma((SINK - 1,)),
            dma, dma,
            pltpu.SemaphoreType.REGULAR,
        ],
        compiler_params=pltpu.CompilerParams(
            collective_id=0, has_side_effects=True, vmem_limit_bytes=48000 * 1024
        ),
    )(*[pltpu.with_memory_space_constraint(a, pltpu.HBM) for a in (maps, weight, proj_weight, prototypes)])


def solution(mesh):
    return jax.shard_map(
        shards,
        mesh=mesh,
        in_specs=(
            P(("dp", "fsdp"), None, None, None, None),
            P(None, None, "fsdp"),
            P(),
            P(None, "fsdp"),
        ),
        out_specs=P(("dp", "fsdp"), None),
        check_vma=False,
    )
```

```python
import jax
import jax.numpy as jnp
from jax import lax
from jax.experimental import pallas as pl
from jax.experimental.pallas import tpu as pltpu
from jax.sharding import PartitionSpec as P

MESH = pl.DeviceIdType.MESH
F32 = jnp.float32
BF16 = jnp.bfloat16

SINK = 3
PROTOS = 3072
EPS = 1e-06
TEMP = 0.05

N = 8
ROWS = 32
MAP = 14 * ROWS
STAGES = ((0, 640), (2560, 512))
HALF = PROTOS // 2
SLICE = 384
GRID = 64
CUBE = 8


def device(x, y, z, c):
    dp = lax.rem(x, N) * 16 + (lax.rem(z, N) // 4) * 8 + lax.rem(y, N)
    return dp, lax.rem(z, 4) * 2 + lax.rem(c, 2)


def nt(a, b):
    return lax.dot_general(a, b, (((1,), (1,)), ((), ())), preferred_element_type=F32)


def split_rows(v):
    hi = v.astype(BF16).astype(F32)
    row = lax.broadcasted_iota(jnp.int32, (16, v.shape[1]), 0)
    return jnp.where(row == 0, hi, jnp.where(row == 1, v - hi, 0.0)).astype(BF16)


def kernel(
    x_hbm, w_hbm, proj_hbm, proto_hbm, out_ref,
    wide, sib, xf, xs, acc, gath, proj, proto, prs, part, zb, ef, eh, cb, rb, fin,
    loc, sib_s, sib_r, p1_s, p1_r, p2_s, p2_r, pr_s, pr_r, pt_s, pt_r,
    d1_s, d1_r, c_s, c_r, r_s, r_r, f_s, f_r, far,
):
    dp, fs = lax.axis_index("dp"), lax.axis_index("fsdp")
    x, y, zh = dp // 16, lax.rem(dp, 8), lax.rem(dp // 8, 2)
    zl, c = fs // 2, lax.rem(fs, 2)
    z = zh * 4 + zl
    sibling = device(x, y, z, c + 1)
    zpeer = [None] + [device(x, y, z + k, c) for k in range(1, N)]
    ypeer = [None] + [device(x, y + k, z, c) for k in range(1, N)]
    xpeer = [None] + [device(x + k, y, z, c) for k in range(1, N)]
    steps = range(0, N, 2)
    grid = [device(x + i, y + j, z + k, c) for i in steps for j in steps for k in steps][1:]
    other = [a + 1 - 2 * lax.rem(a, 2) for a in (x, y, z)]
    cube = []
    for m in range(1, CUBE):
        at = [b if m >> n & 1 else a for n, (a, b) in enumerate(zip((x, y, z), other))]
        cube.append(device(*at, c))

    def send(src, dst, s, r, to):
        pltpu.make_async_remote_copy(
            src_ref=src, dst_ref=dst, send_sem=s, recv_sem=r, device_id=to, device_id_type=MESH
        ).start()

    def wait(ref, sem):
        pltpu.make_async_copy(ref, ref, sem).wait()

    due = []

    def drain():
        for ref, sem in due + late:
            wait(ref, sem)

    late = []
    barrier = pltpu.get_barrier_semaphore()
    near = [p[k] for p in (zpeer, xpeer, ypeer) for k in (1, 7, 2, 6)]
    for to in [sibling] + near:
        pl.semaphore_signal(barrier, inc=1, device_id=to, device_id_type=MESH)

    own = pl.ds(pl.multiple_of(zl * 64, 64), 64)
    pltpu.make_async_copy(w_hbm, gath.at[own], loc.at[0]).start()
    pltpu.make_async_copy(proto_hbm, proto, loc.at[1]).start()
    pltpu.make_async_copy(x_hbm, wide, loc.at[2]).start()
    pltpu.make_async_copy(proj_hbm, proj, loc.at[3]).start()

    pltpu.make_async_copy(proto_hbm, proto, loc.at[1]).wait()
    pw = proto[...].astype(F32)
    norm = jnp.sqrt(jnp.sum(pw * pw, axis=0, keepdims=True) + EPS)
    prs[zl] = (pw / norm).astype(BF16)

    def spread(src, slot):
        xf[...] = jnp.zeros((MAP + 96, 512), F32)
        for h in range(14):
            xf[pl.ds(48 + ROWS * h, 28), :] = src[h].astype(F32).reshape(28, 512)
        for j in range(3):
            xs[slot, j] = xf[pl.ds(14 + 2 * j, 512), :].astype(BF16)

    pltpu.make_async_copy(x_hbm, wide, loc.at[2]).wait()
    wait(gath.at[pl.ds(0, 64), :], loc.at[0])
    pltpu.make_async_copy(proj_hbm, proj, loc.at[3]).wait()

    pl.semaphore_wait(barrier, 1 + len(near))

    color = [lax.rem(x + 2 * y, 4), lax.rem(2 * x + y, 4)]

    def piece(stage, s, h, g=None):
        first, size = STAGES[stage]
        row = s * 64 + h * 32
        rows = pl.ds(pl.multiple_of(row, 32), 32)
        if g is not None:
            rows = pl.ds(pl.multiple_of(row + 16 * g, 16), 16)
        return gath.at[rows, pl.ds(pl.multiple_of(first + color[h] * size, 128), size)]

    for stage in range(2):
        for h in range(2):
            mine = piece(stage, zl, h)
            send(mine, mine, p1_s, p1_r.at[stage, 0, h], zpeer[7])
            send(mine, mine, p1_s, p1_r.at[stage, 2, h], zpeer[1])
        for h in range(2):
            for g, k in ((0, 2), (1, 6)):
                mine = piece(stage, zl, h, g)
                send(mine, mine, p1_s, p1_r.at[stage, 1, h], zpeer[k])
    send(wide, sib, sib_s, sib_r, sibling)
    due.append((gath.at[pl.ds(0, 48), :], p1_s))
    due.append((wide, sib_s))
    late = [(sib, sib_r)]
    for to in near:
        pl.semaphore_signal(far.at[0], inc=1, device_id=to, device_id_type=MESH)

    spread(wide, c)

    def forward(stage, k, h):
        s = lax.rem(zl + k, 4)
        full, half = (xpeer, ypeer) if h == 0 else (ypeer, xpeer)
        whole = piece(stage, s, h)
        wait(whole, p1_r.at[stage, k - 1, h])
        for to in (full[1], full[7]):
            send(whole, whole, p2_s, p2_r.at[stage], to)
        for g, to in ((0, half[1]), (1, half[7])):
            mine = piece(stage, s, h, g)
            send(mine, mine, p2_s, p2_r.at[stage], to)

    for stage in range(2):
        for k, h in ((1, 0), (3, 0), (1, 1), (3, 1), (2, 0), (2, 1)):
            forward(stage, k, h)
        if stage == 0:
            pl.semaphore_wait(far.at[0], len(near))
            for to in (xpeer[2], xpeer[4], xpeer[6], cube[0]):
                pl.semaphore_signal(far.at[1], inc=1, device_id=to, device_id_type=MESH)
    due.append((gath.at[pl.ds(0, 144), :], p2_s))
    late.append((gath.at[pl.ds(0, 80), :], p2_r.at[0]))
    late.append((gath.at[pl.ds(0, 64), :], p2_r.at[1]))
    for to in (zpeer[1], zpeer[7]):
        send(prs.at[zl], prs.at[zl], pr_s, pr_r, to)
    for g, to in ((0, zpeer[2]), (1, zpeer[6])):
        rows = pl.ds(128 * g, 128)
        send(prs.at[zl, rows], prs.at[zl, rows], pr_s, pr_r, to)

    due.append((prs.at[pl.ds(0, 3)], pr_s))
    late.append((prs.at[pl.ds(0, 3)], pr_r))
    wait(*late.pop(0))
    spread(sib, 1 - c)

    o = lax.broadcasted_iota(jnp.int32, (256, 512), 0)
    i = lax.broadcasted_iota(jnp.int32, (256, 512), 1)
    pick = jnp.where(i == (o // 64) * 128 + 64 * c + lax.rem(o, 64), 1.0, 0.0).astype(BF16)
    for slot in range(2):
        acc[slot] = nt(xs[slot, 1, pl.ds(32, MAP), :], pick)

    def conv(taps):
        def maps(slot, carry):
            for t in taps:
                r, j = divmod(t, 3)
                acc[slot] += nt(xs[slot, j, pl.ds(32 * r, MAP), :], gath[:, pl.ds(512 * t, 512)])
            return carry

        lax.fori_loop(0, 2, maps, 0)

    pl.semaphore_wait(far.at[1], 4)
    for to in (zpeer[2], zpeer[4], zpeer[6]):
        pl.semaphore_signal(far.at[2], inc=1, device_id=to, device_id_type=MESH)

    wait(*late.pop(0))
    conv(range(5))
    wait(*late.pop(0))
    conv(range(5, 9))

    row32 = lax.broadcasted_iota(jnp.int32, (ROWS, 256), 0)
    row16 = lax.broadcasted_iota(jnp.int32, (16, 256), 0)
    pooled = jnp.zeros((16, 256), F32)
    for slot in range(2):
        line = jnp.sum(jnp.maximum(acc[slot].reshape(14, ROWS, 256), 0.0), axis=0)
        for b in range(2):
            keep = (lax.rem(row32, 2) == b) & (row32 < 28)
            mean = jnp.sum(jnp.where(keep, line, 0.0), axis=0, keepdims=True) / 196.0
            pooled = jnp.where(lax.rem(row16, 4) == 2 * slot + b, mean, pooled)

    weights = jnp.concatenate(
        [proj[pl.ds(pl.multiple_of(128 * a + 64 * c, 64), 64), :] for a in range(4)], axis=0
    )
    partial = jnp.dot(pooled.astype(BF16), weights, preferred_element_type=F32)
    part[0] = partial[:8]
    send(part.at[0], part.at[1], pt_s, pt_r, sibling)
    due.append((part.at[0], pt_s))
    wait(part.at[1], pt_r)
    projected = part[0] + part[1]
    norm = jnp.sqrt(jnp.sum(projected * projected, axis=1, keepdims=True) + EPS)
    embed = (projected / norm).astype(BF16).astype(F32)

    zb[0] = embed[:4].astype(BF16)
    pl.semaphore_wait(far.at[2], 3)
    for k, to in enumerate(grid):
        send(zb.at[0], zb.at[k + 1], d1_s, d1_r, to)
    due.append((zb.at[pl.ds(1, GRID - 1)], d1_s))
    wait(*late.pop(0))
    wait(zb.at[pl.ds(1, GRID - 1)], d1_r)
    images = zb[...].astype(F32).reshape(256, 256).astype(BF16)
    for a in range(4):
        cols = pl.ds(SLICE * a, SLICE)
        e = jnp.exp(jnp.dot(images, prs[a], preferred_element_type=F32) / TEMP)
        ef[:, cols] = e
        eh[:, cols] = e.astype(BF16)
        cb[0, CUBE - 1, :, cols] = jnp.sum(e, axis=0, keepdims=True)

    for sweep in range(SINK):
        for k, to in enumerate(cube):
            send(cb.at[sweep, CUBE - 1], cb.at[sweep, k], c_s.at[sweep], c_r.at[sweep], to)
        due.append((cb.at[sweep, pl.ds(0, CUBE - 1)], c_s.at[sweep]))
        wait(cb.at[sweep, pl.ds(0, CUBE - 1)], c_r.at[sweep])
        total = cb[sweep, 0]
        for k in range(1, CUBE):
            total = total + cb[sweep, k]
        v = 1.0 / total
        if sweep == SINK - 1:
            break
        vv = split_rows(v)
        s = nt(vv, eh[...])
        rb[sweep, 0] = s[0:1] + s[1:2]
        send(rb.at[sweep, 0], rb.at[sweep, 1], r_s.at[sweep], r_r.at[sweep], sibling)
        due.append((rb.at[sweep, 0], r_s.at[sweep]))
        wait(rb.at[sweep, 1], r_r.at[sweep])
        uu = split_rows(1.0 / (rb[sweep, 0] + rb[sweep, 1]))
        s = jnp.dot(uu, eh[...], preferred_element_type=F32)
        cb[sweep + 1, CUBE - 1] = s[0:1] + s[1:2]

    fin[0] = ef[pl.ds(0, 8), :] * v
    send(fin.at[0], fin.at[1], f_s, f_r, sibling)
    due.append((fin.at[0], f_s))
    wait(fin.at[1], f_r)
    even = jnp.where(c == 0, fin[0], fin[1])
    odd = jnp.where(c == 0, fin[1], fin[0])
    rows = jnp.sum(even, axis=1, keepdims=True) + jnp.sum(odd, axis=1, keepdims=True)
    scale = PROTOS / rows
    even, odd = even * scale, odd * scale
    first = 2 * c
    rowc = lax.broadcasted_iota(jnp.int32, (8, SLICE), 0)
    for b in range(2):
        for a in range(4):
            for half, codes in ((0, even), (1, odd)):
                mine = jnp.where(rowc == first + b, codes[:, SLICE * a : SLICE * (a + 1)], 0.0)
                out_ref[pl.ds(b, 1), pl.ds(SLICE * (2 * a + half), SLICE)] = jnp.sum(
                    mine, axis=0, keepdims=True
                )

    drain()


def shards(features, conv_weight, proj_weight, prototypes):
    maps = jnp.transpose(features[:, :, :, 0, :], (1, 2, 0, 3))
    weight = jnp.transpose(conv_weight[0])
    dma = pltpu.SemaphoreType.DMA
    return pl.pallas_call(
        kernel,
        out_shape=jax.ShapeDtypeStruct((2, PROTOS), F32),
        in_specs=[pl.BlockSpec(memory_space=pltpu.HBM)] * 4,
        out_specs=pl.BlockSpec(memory_space=pltpu.VMEM),
        scratch_shapes=[
            pltpu.VMEM((14, 14, 2, 512), BF16),
            pltpu.VMEM((14, 14, 2, 512), BF16),
            pltpu.VMEM((MAP + 96, 512), F32),
            pltpu.VMEM((2, 3, 512, 512), BF16),
            pltpu.VMEM((2, MAP, 256), F32),
            pltpu.VMEM((256, 4608), BF16),
            pltpu.VMEM((512, 256), BF16),
            pltpu.VMEM((256, SLICE), BF16),
            pltpu.VMEM((4, 256, SLICE), BF16),
            pltpu.VMEM((2, 8, 256), F32),
            pltpu.VMEM((GRID, 4, 256), BF16),
            pltpu.VMEM((256, HALF), F32),
            pltpu.VMEM((256, HALF), BF16),
            pltpu.VMEM((SINK, CUBE, 1, HALF), F32),
            pltpu.VMEM((SINK - 1, 2, 1, 256), F32),
            pltpu.VMEM((2, 8, HALF), F32),
            dma((4,)),
            dma, dma,
            dma, dma((2, 3, 2)),
            dma, dma((2,)),
            dma, dma,
            dma, dma,
            dma, dma,
            dma((SINK,)), dma((SINK,)),
            dma((SINK - 1,)), dma((SINK - 1,)),
            dma, dma,
            pltpu.SemaphoreType.REGULAR((3,)),
        ],
        compiler_params=pltpu.CompilerParams(
            collective_id=0, has_side_effects=True, vmem_limit_bytes=48000 * 1024
        ),
    )(*[pltpu.with_memory_space_constraint(a, pltpu.HBM) for a in (maps, weight, proj_weight, prototypes)])


def solution(mesh):
    return jax.shard_map(
        shards,
        mesh=mesh,
        in_specs=(
            P(("dp", "fsdp"), None, None, None, None),
            P(None, None, "fsdp"),
            P(),
            P(None, "fsdp"),
        ),
        out_specs=P(("dp", "fsdp"), None),
        check_vma=False,
    )
```

```python
import jax
import jax.numpy as jnp
from jax import lax
from jax.experimental import pallas as pl
from jax.experimental.pallas import tpu as pltpu
from jax.sharding import PartitionSpec as P

MESH = pl.DeviceIdType.MESH
F32 = jnp.float32
BF16 = jnp.bfloat16

SINK = 3
PROTOS = 3072
EPS = 1e-06
TEMP = 0.05

N = 8
ROWS = 32
MAP = 14 * ROWS
STAGES = ((0, 640), (2560, 512))
HALF = PROTOS // 2
SLICE = 384
GRID = 64
CUBE = 8


def device(x, y, z, c):
    dp = lax.rem(x, N) * 16 + (lax.rem(z, N) // 4) * 8 + lax.rem(y, N)
    return dp, lax.rem(z, 4) * 2 + lax.rem(c, 2)


def nt(a, b):
    return lax.dot_general(a, b, (((1,), (1,)), ((), ())), preferred_element_type=F32)


def split_rows(v):
    hi = v.astype(BF16).astype(F32)
    row = lax.broadcasted_iota(jnp.int32, (16, v.shape[1]), 0)
    return jnp.where(row == 0, hi, jnp.where(row == 1, v - hi, 0.0)).astype(BF16)


def kernel(
    x_hbm, w_hbm, proj_hbm, proto_hbm, out_ref,
    wide, sib, xf, xs, acc, gath, proj, proto, prs, part, zb, ef, eh, cb, rb, fin,
    loc, sib_s, sib_r, p1_s, p1_r, p2_s, p2_r, p3_s, pr_s, pr_r, pt_s, pt_r,
    d1_s, d1_r, c_s, c_r, r_s, r_r, f_s, f_r, far,
):
    dp, fs = lax.axis_index("dp"), lax.axis_index("fsdp")
    x, y, zh = dp // 16, lax.rem(dp, 8), lax.rem(dp // 8, 2)
    zl, c = fs // 2, lax.rem(fs, 2)
    z = zh * 4 + zl
    sibling = device(x, y, z, c + 1)
    zpeer = [None] + [device(x, y, z + k, c) for k in range(1, N)]
    ypeer = [None] + [device(x, y + k, z, c) for k in range(1, N)]
    xpeer = [None] + [device(x + k, y, z, c) for k in range(1, N)]
    steps = range(0, N, 2)
    grid = [(i, j, k) for i in steps for j in steps for k in steps][1:]
    grid.sort(key=lambda step: -sum(min(a, N - a) for a in step))
    grid = [device(x + i, y + j, z + k, c) for i, j, k in grid]
    other = [a + 1 - 2 * lax.rem(a, 2) for a in (x, y, z)]
    cube = []
    for m in (7, 6, 5, 3, 4, 2, 1):
        at = [b if m >> n & 1 else a for n, (a, b) in enumerate(zip((x, y, z), other))]
        cube.append(device(*at, c))

    def send(src, dst, s, r, to):
        pltpu.make_async_remote_copy(
            src_ref=src, dst_ref=dst, send_sem=s, recv_sem=r, device_id=to, device_id_type=MESH
        ).start()

    def wait(ref, sem):
        pltpu.make_async_copy(ref, ref, sem).wait()

    due = []

    def drain():
        for ref, sem in due + late:
            wait(ref, sem)

    late = []
    barrier = pltpu.get_barrier_semaphore()
    near = [p[k] for p in (zpeer, xpeer, ypeer) for k in (1, 7, 2, 6)]
    for to in [sibling] + near:
        pl.semaphore_signal(barrier, inc=1, device_id=to, device_id_type=MESH)

    own = pl.ds(pl.multiple_of(zl * 64, 64), 64)
    pltpu.make_async_copy(w_hbm, gath.at[own], loc.at[0]).start()
    pltpu.make_async_copy(proto_hbm, proto, loc.at[1]).start()
    pltpu.make_async_copy(x_hbm, wide, loc.at[2]).start()
    pltpu.make_async_copy(proj_hbm, proj, loc.at[3]).start()

    pltpu.make_async_copy(proto_hbm, proto, loc.at[1]).wait()
    pw = proto[...].astype(F32)
    norm = jnp.sqrt(jnp.sum(pw * pw, axis=0, keepdims=True) + EPS)
    prs[zl] = (pw / norm).astype(BF16)

    def spread(src, slot):
        xf[...] = jnp.zeros((MAP + 96, 512), F32)
        for h in range(14):
            xf[pl.ds(48 + ROWS * h, 28), :] = src[h].astype(F32).reshape(28, 512)
        for j in range(3):
            xs[slot, j] = xf[pl.ds(14 + 2 * j, 512), :].astype(BF16)

    pltpu.make_async_copy(x_hbm, wide, loc.at[2]).wait()
    wait(gath.at[pl.ds(0, 64), :], loc.at[0])
    pltpu.make_async_copy(proj_hbm, proj, loc.at[3]).wait()

    pl.semaphore_wait(barrier, 1 + len(near))

    color = [lax.rem(x + 2 * y, 4), lax.rem(2 * x + y, 4)]

    def piece(stage, s, h, g=None, ahead=0):
        first, size = STAGES[stage]
        hue = lax.rem(color[h] + ahead, 4)
        row = s * 64 + h * 32
        rows = pl.ds(pl.multiple_of(row, 32), 32)
        if g is not None:
            rows = pl.ds(pl.multiple_of(row + 16 * g, 16), 16)
        return gath.at[rows, pl.ds(pl.multiple_of(first + hue * size, 128), size)]

    for stage in range(2):
        for h in range(2):
            mine = piece(stage, zl, h)
            send(mine, mine, p1_s, p1_r.at[stage, 0, h], zpeer[7])
            send(mine, mine, p1_s, p1_r.at[stage, 2, h], zpeer[1])
        for h in range(2):
            for g, k in ((0, 2), (1, 6)):
                mine = piece(stage, zl, h, g)
                send(mine, mine, p1_s, p1_r.at[stage, 1, h], zpeer[k])
    for h in range(2):
        mine = piece(1, zl, h, ahead=2)
        send(mine, mine, p3_s, p2_r.at[1], zpeer[7])
        send(mine, mine, p3_s, p2_r.at[1], zpeer[1])
        for g, k in ((0, 2), (1, 6)):
            mine = piece(1, zl, h, g, ahead=2)
            send(mine, mine, p3_s, p2_r.at[1], zpeer[k])
    send(wide, sib, sib_s, sib_r, sibling)
    due.append((gath.at[pl.ds(0, 48), :], p1_s))
    due.append((wide, sib_s))
    late = [(sib, sib_r)]
    for to in near:
        pl.semaphore_signal(far.at[0], inc=1, device_id=to, device_id_type=MESH)

    spread(wide, c)

    def forward(stage, k, h):
        s = lax.rem(zl + k, 4)
        full, half = (xpeer, ypeer) if h == 0 else (ypeer, xpeer)
        whole = piece(stage, s, h)
        wait(whole, p1_r.at[stage, k - 1, h])
        for to in (full[1], full[7]):
            send(whole, whole, p2_s.at[stage], p2_r.at[stage], to)
        if stage == 0:
            for g, to in ((0, half[1]), (1, half[7])):
                mine = piece(stage, s, h, g)
                send(mine, mine, p2_s.at[stage], p2_r.at[stage], to)

    for stage in range(2):
        for k, h in ((1, 0), (3, 0), (1, 1), (3, 1), (2, 0), (2, 1)):
            forward(stage, k, h)
        if stage == 0:
            pl.semaphore_wait(far.at[0], len(near))
            for to in (xpeer[2], xpeer[4], xpeer[6], cube[6]):
                pl.semaphore_signal(far.at[1], inc=1, device_id=to, device_id_type=MESH)
    due.append((gath.at[pl.ds(0, 80), :], p2_s.at[0]))
    due.append((gath.at[:, pl.ds(0, 768)], p2_s.at[1]))
    due.append((gath.at[pl.ds(0, 192), pl.ds(0, 512)], p3_s))
    late.append((gath.at[pl.ds(0, 80), :], p2_r.at[0]))
    late.append((gath.at[pl.ds(0, 64), :], p2_r.at[1]))
    for to in (zpeer[1], zpeer[7]):
        send(prs.at[zl], prs.at[zl], pr_s, pr_r, to)
    for g, to in ((0, zpeer[2]), (1, zpeer[6])):
        rows = pl.ds(128 * g, 128)
        send(prs.at[zl, rows], prs.at[zl, rows], pr_s, pr_r, to)

    due.append((prs.at[pl.ds(0, 3)], pr_s))
    late.append((prs.at[pl.ds(0, 3)], pr_r))
    wait(*late.pop(0))
    spread(sib, 1 - c)

    o = lax.broadcasted_iota(jnp.int32, (256, 512), 0)
    i = lax.broadcasted_iota(jnp.int32, (256, 512), 1)
    pick = jnp.where(i == (o // 64) * 128 + 64 * c + lax.rem(o, 64), 1.0, 0.0).astype(BF16)
    for slot in range(2):
        acc[slot] = nt(xs[slot, 1, pl.ds(32, MAP), :], pick)

    def conv(taps):
        def maps(slot, carry):
            for t in taps:
                r, j = divmod(t, 3)
                acc[slot] += nt(xs[slot, j, pl.ds(32 * r, MAP), :], gath[:, pl.ds(512 * t, 512)])
            return carry

        lax.fori_loop(0, 2, maps, 0)

    pl.semaphore_wait(far.at[1], 4)
    for to in (zpeer[2], zpeer[4], zpeer[6]):
        pl.semaphore_signal(far.at[2], inc=1, device_id=to, device_id_type=MESH)

    wait(*late.pop(0))
    conv(range(5))
    wait(*late.pop(0))
    conv(range(5, 9))

    row32 = lax.broadcasted_iota(jnp.int32, (ROWS, 256), 0)
    row16 = lax.broadcasted_iota(jnp.int32, (16, 256), 0)
    pooled = jnp.zeros((16, 256), F32)
    for slot in range(2):
        line = jnp.sum(jnp.maximum(acc[slot].reshape(14, ROWS, 256), 0.0), axis=0)
        for b in range(2):
            keep = (lax.rem(row32, 2) == b) & (row32 < 28)
            mean = jnp.sum(jnp.where(keep, line, 0.0), axis=0, keepdims=True) / 196.0
            pooled = jnp.where(lax.rem(row16, 4) == 2 * slot + b, mean, pooled)

    weights = jnp.concatenate(
        [proj[pl.ds(pl.multiple_of(128 * a + 64 * c, 64), 64), :] for a in range(4)], axis=0
    )
    partial = jnp.dot(pooled.astype(BF16), weights, preferred_element_type=F32)
    part[0] = partial[:8]
    send(part.at[0], part.at[1], pt_s, pt_r, sibling)
    due.append((part.at[0], pt_s))
    wait(part.at[1], pt_r)
    projected = part[0] + part[1]
    norm = jnp.sqrt(jnp.sum(projected * projected, axis=1, keepdims=True) + EPS)
    embed = (projected / norm).astype(BF16).astype(F32)

    zb[0] = embed[:4].astype(BF16)
    pl.semaphore_wait(far.at[2], 3)
    for k, to in enumerate(grid):
        send(zb.at[0], zb.at[k + 1], d1_s, d1_r, to)
    due.append((zb.at[pl.ds(1, GRID - 1)], d1_s))
    wait(*late.pop(0))
    wait(zb.at[pl.ds(1, GRID - 1)], d1_r)
    images = zb[...].astype(F32).reshape(256, 256).astype(BF16)
    for a in range(4):
        cols = pl.ds(SLICE * a, SLICE)
        e = jnp.exp(jnp.dot(images, prs[a], preferred_element_type=F32) / TEMP)
        ef[:, cols] = e
        eh[:, cols] = e.astype(BF16)
        cb[0, CUBE - 1, :, cols] = jnp.sum(e, axis=0, keepdims=True)

    for sweep in range(SINK):
        for k, to in enumerate(cube):
            send(cb.at[sweep, CUBE - 1], cb.at[sweep, k], c_s.at[sweep], c_r.at[sweep], to)
        due.append((cb.at[sweep, pl.ds(0, CUBE - 1)], c_s.at[sweep]))
        wait(cb.at[sweep, pl.ds(0, CUBE - 1)], c_r.at[sweep])
        total = cb[sweep, 0]
        for k in range(1, CUBE):
            total = total + cb[sweep, k]
        v = 1.0 / total
        if sweep == SINK - 1:
            break
        vv = split_rows(v)
        s = nt(vv, eh[...])
        rb[sweep, 0] = s[0:1] + s[1:2]
        send(rb.at[sweep, 0], rb.at[sweep, 1], r_s.at[sweep], r_r.at[sweep], sibling)
        due.append((rb.at[sweep, 0], r_s.at[sweep]))
        wait(rb.at[sweep, 1], r_r.at[sweep])
        uu = split_rows(1.0 / (rb[sweep, 0] + rb[sweep, 1]))
        s = jnp.dot(uu, eh[...], preferred_element_type=F32)
        cb[sweep + 1, CUBE - 1] = s[0:1] + s[1:2]

    fin[0] = ef[pl.ds(0, 8), :][:4] * v
    send(fin.at[0], fin.at[1], f_s, f_r, sibling)
    due.append((fin.at[0], f_s))
    wait(fin.at[1], f_r)
    even = jnp.where(c == 0, fin[0], fin[1])
    odd = jnp.where(c == 0, fin[1], fin[0])
    rows = jnp.sum(even, axis=1, keepdims=True) + jnp.sum(odd, axis=1, keepdims=True)
    scale = PROTOS / rows
    even, odd = even * scale, odd * scale
    first = 2 * c
    rowc = lax.broadcasted_iota(jnp.int32, (4, SLICE), 0)
    for b in range(2):
        for a in range(4):
            for half, codes in ((0, even), (1, odd)):
                mine = jnp.where(rowc == first + b, codes[:, SLICE * a : SLICE * (a + 1)], 0.0)
                out_ref[pl.ds(b, 1), pl.ds(SLICE * (2 * a + half), SLICE)] = jnp.sum(
                    mine, axis=0, keepdims=True
                )

    drain()


def shards(features, conv_weight, proj_weight, prototypes):
    maps = jnp.transpose(features[:, :, :, 0, :], (1, 2, 0, 3))
    weight = jnp.transpose(conv_weight[0])
    dma = pltpu.SemaphoreType.DMA
    return pl.pallas_call(
        kernel,
        out_shape=jax.ShapeDtypeStruct((2, PROTOS), F32),
        in_specs=[pl.BlockSpec(memory_space=pltpu.HBM)] * 4,
        out_specs=pl.BlockSpec(memory_space=pltpu.VMEM),
        scratch_shapes=[
            pltpu.VMEM((14, 14, 2, 512), BF16),
            pltpu.VMEM((14, 14, 2, 512), BF16),
            pltpu.VMEM((MAP + 96, 512), F32),
            pltpu.VMEM((2, 3, 512, 512), BF16),
            pltpu.VMEM((2, MAP, 256), F32),
            pltpu.VMEM((256, 4608), BF16),
            pltpu.VMEM((512, 256), BF16),
            pltpu.VMEM((256, SLICE), BF16),
            pltpu.VMEM((4, 256, SLICE), BF16),
            pltpu.VMEM((2, 8, 256), F32),
            pltpu.VMEM((GRID, 4, 256), BF16),
            pltpu.VMEM((256, HALF), F32),
            pltpu.VMEM((256, HALF), BF16),
            pltpu.VMEM((SINK, CUBE, 1, HALF), F32),
            pltpu.VMEM((SINK - 1, 2, 1, 256), F32),
            pltpu.VMEM((2, 4, HALF), F32),
            dma((4,)),
            dma, dma,
            dma, dma((2, 3, 2)),
            dma((2,)), dma((2,)), dma,
            dma, dma,
            dma, dma,
            dma, dma,
            dma((SINK,)), dma((SINK,)),
            dma((SINK - 1,)), dma((SINK - 1,)),
            dma, dma,
            pltpu.SemaphoreType.REGULAR((3,)),
        ],
        compiler_params=pltpu.CompilerParams(
            collective_id=0, has_side_effects=True, vmem_limit_bytes=48000 * 1024
        ),
    )(*[pltpu.with_memory_space_constraint(a, pltpu.HBM) for a in (maps, weight, proj_weight, prototypes)])


def solution(mesh):
    return jax.shard_map(
        shards,
        mesh=mesh,
        in_specs=(
            P(("dp", "fsdp"), None, None, None, None),
            P(None, None, "fsdp"),
            P(),
            P(None, "fsdp"),
        ),
        out_specs=P(("dp", "fsdp"), None),
        check_vma=False,
    )
```

```python
import jax
import jax.numpy as jnp
from jax import lax
from jax.experimental import pallas as pl
from jax.experimental.pallas import tpu as pltpu
from jax.sharding import PartitionSpec as P

MESH = pl.DeviceIdType.MESH
F32 = jnp.float32
BF16 = jnp.bfloat16

SINK = 3
PROTOS = 3072
EPS = 1e-06
TEMP = 0.05

N = 8
ROWS = 32
MAP = 14 * ROWS
STAGES = ((0, 512), (2048, 384), (3584, 256))
DIRECT = 1
HALF = PROTOS // 2
SLICE = 384
GRID = 64
CUBE = 8


def device(x, y, z, c):
    dp = lax.rem(x, N) * 16 + (lax.rem(z, N) // 4) * 8 + lax.rem(y, N)
    return dp, lax.rem(z, 4) * 2 + lax.rem(c, 2)


def nt(a, b):
    return lax.dot_general(a, b, (((1,), (1,)), ((), ())), preferred_element_type=F32)


def split_rows(v):
    hi = v.astype(BF16).astype(F32)
    row = lax.broadcasted_iota(jnp.int32, (16, v.shape[1]), 0)
    return jnp.where(row == 0, hi, jnp.where(row == 1, v - hi, 0.0)).astype(BF16)


def kernel(
    x_hbm, w_hbm, proj_hbm, proto_hbm, out_ref,
    wide, sib, xf, xs, acc, gath, proj, proto, prs, part, zb, ef, eh, cb, rb, fin,
    loc, sib_s, sib_r, p1_s, p1_r, p2_s, p2_r, p3_s, pr_s, pr_r, pt_s, pt_r,
    d1_s, d1_r, c_s, c_r, r_s, r_r, f_s, f_r, far,
):
    dp, fs = lax.axis_index("dp"), lax.axis_index("fsdp")
    x, y, zh = dp // 16, lax.rem(dp, 8), lax.rem(dp // 8, 2)
    zl, c = fs // 2, lax.rem(fs, 2)
    z = zh * 4 + zl
    sibling = device(x, y, z, c + 1)
    zpeer = [None] + [device(x, y, z + k, c) for k in range(1, N)]
    ypeer = [None] + [device(x, y + k, z, c) for k in range(1, N)]
    xpeer = [None] + [device(x + k, y, z, c) for k in range(1, N)]
    steps = range(0, N, 2)
    grid = [(i, j, k) for i in steps for j in steps for k in steps][1:]
    grid.sort(key=lambda step: -sum(min(a, N - a) for a in step))
    grid = [device(x + i, y + j, z + k, c) for i, j, k in grid]
    other = [a + 1 - 2 * lax.rem(a, 2) for a in (x, y, z)]
    cube, cross = [], []
    for m in (7, 6, 5, 3, 4, 2, 1):
        at = [b if m >> n & 1 else a for n, (a, b) in enumerate(zip((x, y, z), other))]
        cube.append(device(*at, c))
        cross.append(device(*at, c + 1))

    def send(src, dst, s, r, to):
        pltpu.make_async_remote_copy(
            src_ref=src, dst_ref=dst, send_sem=s, recv_sem=r, device_id=to, device_id_type=MESH
        ).start()

    def wait(ref, sem):
        pltpu.make_async_copy(ref, ref, sem).wait()

    due = []

    def drain():
        for ref, sem in due + late:
            wait(ref, sem)

    late = []
    barrier = pltpu.get_barrier_semaphore()
    near = [p[k] for p in (zpeer, xpeer, ypeer) for k in (1, 7, 2, 6)]
    for to in [sibling] + near:
        pl.semaphore_signal(barrier, inc=1, device_id=to, device_id_type=MESH)

    own = pl.ds(pl.multiple_of(zl * 64, 64), 64)
    pltpu.make_async_copy(w_hbm, gath.at[own], loc.at[0]).start()
    pltpu.make_async_copy(proto_hbm, proto, loc.at[1]).start()
    pltpu.make_async_copy(x_hbm, wide, loc.at[2]).start()
    pltpu.make_async_copy(proj_hbm, proj, loc.at[3]).start()

    pltpu.make_async_copy(proto_hbm, proto, loc.at[1]).wait()
    pw = proto[...].astype(F32)
    norm = jnp.sqrt(jnp.sum(pw * pw, axis=0, keepdims=True) + EPS)
    prs[zl] = (pw / norm).astype(BF16)

    def spread(src, slot):
        xf[...] = jnp.zeros((MAP + 96, 512), F32)
        for h in range(14):
            xf[pl.ds(48 + ROWS * h, 28), :] = src[h].astype(F32).reshape(28, 512)
        for j in range(3):
            xs[slot, j] = xf[pl.ds(14 + 2 * j, 512), :].astype(BF16)

    pltpu.make_async_copy(x_hbm, wide, loc.at[2]).wait()
    wait(gath.at[pl.ds(0, 64), :], loc.at[0])
    pltpu.make_async_copy(proj_hbm, proj, loc.at[3]).wait()

    pl.semaphore_wait(barrier, 1 + len(near))

    color = [lax.rem(x + 2 * y, 4), lax.rem(2 * x + y, 4)]

    def piece(stage, s, h, g=None, ahead=0):
        first, size = STAGES[stage]
        hue = lax.rem(color[h] + ahead, 4)
        row = s * 64 + h * 32
        rows = pl.ds(pl.multiple_of(row, 32), 32)
        if g is not None:
            rows = pl.ds(pl.multiple_of(row + 16 * g, 16), 16)
        return gath.at[rows, pl.ds(pl.multiple_of(first + hue * size, 128), size)]

    for stage in range(3):
        for h in range(2):
            mine = piece(stage, zl, h)
            send(mine, mine, p1_s, p1_r.at[stage, 0, h], zpeer[7])
            send(mine, mine, p1_s, p1_r.at[stage, 2, h], zpeer[1])
        for h in range(2):
            for g, k in ((0, 2), (1, 6)):
                mine = piece(stage, zl, h, g)
                send(mine, mine, p1_s, p1_r.at[stage, 1, h], zpeer[k])
    for h in range(2):
        mine = piece(DIRECT, zl, h, ahead=2)
        send(mine, mine, p3_s, p2_r.at[DIRECT], zpeer[7])
        send(mine, mine, p3_s, p2_r.at[DIRECT], zpeer[1])
        for g, k in ((0, 2), (1, 6)):
            mine = piece(DIRECT, zl, h, g, ahead=2)
            send(mine, mine, p3_s, p2_r.at[DIRECT], zpeer[k])
    send(wide, sib, sib_s, sib_r, sibling)
    due.append((gath.at[pl.ds(0, 48), :], p1_s))
    due.append((wide, sib_s))
    late = [(sib, sib_r)]
    for to in near:
        pl.semaphore_signal(far.at[0], inc=1, device_id=to, device_id_type=MESH)

    spread(wide, c)

    def forward(stage, k, h):
        s = lax.rem(zl + k, 4)
        full, half = (xpeer, ypeer) if h == 0 else (ypeer, xpeer)
        whole = piece(stage, s, h)
        wait(whole, p1_r.at[stage, k - 1, h])
        for to in (full[1], full[7]):
            send(whole, whole, p2_s.at[stage], p2_r.at[stage], to)
        if stage != DIRECT:
            for g, to in ((0, half[1]), (1, half[7])):
                mine = piece(stage, s, h, g)
                send(mine, mine, p2_s.at[stage], p2_r.at[stage], to)

    for stage in range(3):
        for k, h in ((1, 0), (3, 0), (1, 1), (3, 1), (2, 0), (2, 1)):
            forward(stage, k, h)
        if stage == 0:
            pl.semaphore_wait(far.at[0], len(near))
            for to in (xpeer[2], xpeer[4], xpeer[6], cube[6]):
                pl.semaphore_signal(far.at[1], inc=1, device_id=to, device_id_type=MESH)
    for stage, (sent, came) in enumerate(((64, 64), (32, 48), (32, 32))):
        due.append((gath.at[pl.ds(0, sent), :], p2_s.at[stage]))
        late.append((gath.at[pl.ds(0, came), :], p2_r.at[stage]))
    due.append((gath.at[pl.ds(0, 16), :], p3_s))
    for to in (zpeer[1], zpeer[7]):
        send(prs.at[zl], prs.at[zl], pr_s, pr_r, to)
    for g, to in ((0, zpeer[2]), (1, zpeer[6])):
        rows = pl.ds(128 * g, 128)
        send(prs.at[zl, rows], prs.at[zl, rows], pr_s, pr_r, to)

    due.append((prs.at[pl.ds(0, 3)], pr_s))
    late.append((prs.at[pl.ds(0, 3)], pr_r))
    wait(*late.pop(0))
    spread(sib, 1 - c)

    o = lax.broadcasted_iota(jnp.int32, (256, 512), 0)
    i = lax.broadcasted_iota(jnp.int32, (256, 512), 1)
    pick = jnp.where(i == (o // 64) * 128 + 64 * c + lax.rem(o, 64), 1.0, 0.0).astype(BF16)
    for slot in range(2):
        acc[slot] = nt(xs[slot, 1, pl.ds(32, MAP), :], pick)

    pl.semaphore_wait(far.at[1], 4)
    for to in (zpeer[2], zpeer[4], zpeer[6], sibling):
        pl.semaphore_signal(far.at[2], inc=1, device_id=to, device_id_type=MESH)

    for taps in (range(4), range(4, 7), range(7, 9)):
        wait(*late.pop(0))
        for slot in range(2):
            total = acc[slot]
            for t in taps:
                r, j = divmod(t, 3)
                maps = xs[slot, j, pl.ds(32 * r, MAP), :]
                total = total + nt(maps, gath[:, pl.ds(512 * t, 512)])
            acc[slot] = total

    row32 = lax.broadcasted_iota(jnp.int32, (ROWS, 256), 0)
    row16 = lax.broadcasted_iota(jnp.int32, (16, 256), 0)
    pooled = jnp.zeros((16, 256), F32)
    for slot in range(2):
        line = jnp.sum(jnp.maximum(acc[slot].reshape(14, ROWS, 256), 0.0), axis=0)
        for b in range(2):
            keep = (lax.rem(row32, 2) == b) & (row32 < 28)
            mean = jnp.sum(jnp.where(keep, line, 0.0), axis=0, keepdims=True) / 196.0
            pooled = jnp.where(lax.rem(row16, 4) == 2 * slot + b, mean, pooled)

    weights = jnp.concatenate(
        [proj[pl.ds(pl.multiple_of(128 * a + 64 * c, 64), 64), :] for a in range(4)], axis=0
    )
    partial = jnp.dot(pooled.astype(BF16), weights, preferred_element_type=F32)
    part[0] = partial[:8]
    send(part.at[0], part.at[1], pt_s, pt_r, sibling)
    due.append((part.at[0], pt_s))
    wait(part.at[1], pt_r)
    projected = part[0] + part[1]
    norm = jnp.sqrt(jnp.sum(projected * projected, axis=1, keepdims=True) + EPS)
    embed = (projected / norm).astype(BF16).astype(F32)

    zb[0] = embed[:4].astype(BF16)
    pl.semaphore_wait(far.at[2], 4)
    for k, to in enumerate(grid):
        send(zb.at[0], zb.at[k + 1], d1_s, d1_r, to)
    due.append((zb.at[pl.ds(1, GRID - 1)], d1_s))
    wait(*late.pop(0))
    wait(zb.at[pl.ds(1, GRID - 1)], d1_r)
    images = zb[...].astype(F32).reshape(256, 256).astype(BF16)
    for a in range(4):
        cols = pl.ds(SLICE * a, SLICE)
        e = jnp.exp(jnp.dot(images, prs[a], preferred_element_type=F32) / TEMP)
        ef[:, cols] = e
        eh[:, cols] = e.astype(BF16)
        cb[0, CUBE - 1, :, cols] = jnp.sum(e, axis=0, keepdims=True)

    def total_of(sums):
        total = sums[0]
        for k in range(1, CUBE):
            total = total + sums[k]
        return total

    for sweep in range(SINK - 1):
        sums = cb.at[sweep]
        for k, to in enumerate(cube):
            send(sums.at[CUBE - 1], sums.at[k], c_s.at[sweep], c_r.at[sweep], to)
        due.append((sums.at[pl.ds(0, CUBE - 1)], c_s.at[sweep]))
        if sweep == 0:
            fin[0] = ef[pl.ds(0, 8), :][:4]
            send(fin.at[0], fin.at[1], f_s, f_r, sibling)
            due.append((fin.at[0], f_s))
        wait(sums.at[pl.ds(0, CUBE - 1)], c_r.at[sweep])
        v = 1.0 / total_of(sums)
        vv = split_rows(v)
        s = nt(vv, eh[...])
        rb[sweep, 0] = s[0:1] + s[1:2]
        send(rb.at[sweep, 0], rb.at[sweep, 1], r_s.at[sweep], r_r.at[sweep], sibling)
        due.append((rb.at[sweep, 0], r_s.at[sweep]))
        wait(rb.at[sweep, 1], r_r.at[sweep])
        uu = split_rows(1.0 / (rb[sweep, 0] + rb[sweep, 1]))
        s = jnp.dot(uu, eh[...], preferred_element_type=F32)
        cb[sweep + 1, CUBE - 1] = s[0:1] + s[1:2]

    sums, theirs = cb.at[2], cb.at[3]
    for k in range(CUBE - 1):
        send(sums.at[CUBE - 1], sums.at[k], c_s.at[2], c_r.at[2], cube[k])
        send(sums.at[CUBE - 1], theirs.at[k], c_s.at[3], c_r.at[3], cross[k])
    send(sums.at[CUBE - 1], theirs.at[CUBE - 1], c_s.at[3], c_r.at[3], sibling)
    due.append((sums.at[pl.ds(0, CUBE - 1)], c_s.at[2]))
    due.append((theirs, c_s.at[3]))
    wait(fin.at[1], f_r)
    wait(sums.at[pl.ds(0, CUBE - 1)], c_r.at[2])
    wait(theirs, c_r.at[3])
    here = fin[0] * (1.0 / total_of(sums))
    there = fin[1] * (1.0 / total_of(theirs))
    even = jnp.where(c == 0, here, there)
    odd = jnp.where(c == 0, there, here)
    rows = jnp.sum(even, axis=1, keepdims=True) + jnp.sum(odd, axis=1, keepdims=True)
    scale = PROTOS / rows
    even, odd = even * scale, odd * scale
    first = 2 * c
    rowc = lax.broadcasted_iota(jnp.int32, (4, SLICE), 0)
    for b in range(2):
        for a in range(4):
            for half, codes in ((0, even), (1, odd)):
                mine = jnp.where(rowc == first + b, codes[:, SLICE * a : SLICE * (a + 1)], 0.0)
                out_ref[pl.ds(b, 1), pl.ds(SLICE * (2 * a + half), SLICE)] = jnp.sum(
                    mine, axis=0, keepdims=True
                )

    drain()


def shards(features, conv_weight, proj_weight, prototypes):
    maps = jnp.transpose(features[:, :, :, 0, :], (1, 2, 0, 3))
    weight = jnp.transpose(conv_weight[0])
    dma = pltpu.SemaphoreType.DMA
    return pl.pallas_call(
        kernel,
        out_shape=jax.ShapeDtypeStruct((2, PROTOS), F32),
        in_specs=[pl.BlockSpec(memory_space=pltpu.HBM)] * 4,
        out_specs=pl.BlockSpec(memory_space=pltpu.VMEM),
        scratch_shapes=[
            pltpu.VMEM((14, 14, 2, 512), BF16),
            pltpu.VMEM((14, 14, 2, 512), BF16),
            pltpu.VMEM((MAP + 96, 512), F32),
            pltpu.VMEM((2, 3, 512, 512), BF16),
            pltpu.VMEM((2, MAP, 256), F32),
            pltpu.VMEM((256, 4608), BF16),
            pltpu.VMEM((512, 256), BF16),
            pltpu.VMEM((256, SLICE), BF16),
            pltpu.VMEM((4, 256, SLICE), BF16),
            pltpu.VMEM((2, 8, 256), F32),
            pltpu.VMEM((GRID, 4, 256), BF16),
            pltpu.VMEM((256, HALF), F32),
            pltpu.VMEM((256, HALF), BF16),
            pltpu.VMEM((SINK + 1, CUBE, 1, HALF), F32),
            pltpu.VMEM((SINK - 1, 2, 1, 256), F32),
            pltpu.VMEM((2, 4, HALF), F32),
            dma((4,)),
            dma, dma,
            dma, dma((3, 3, 2)),
            dma((3,)), dma((3,)), dma,
            dma, dma,
            dma, dma,
            dma, dma,
            dma((SINK + 1,)), dma((SINK + 1,)),
            dma((SINK - 1,)), dma((SINK - 1,)),
            dma, dma,
            pltpu.SemaphoreType.REGULAR((3,)),
        ],
        compiler_params=pltpu.CompilerParams(
            collective_id=0, has_side_effects=True, vmem_limit_bytes=48000 * 1024
        ),
    )(*[pltpu.with_memory_space_constraint(a, pltpu.HBM) for a in (maps, weight, proj_weight, prototypes)])


def solution(mesh):
    return jax.shard_map(
        shards,
        mesh=mesh,
        in_specs=(
            P(("dp", "fsdp"), None, None, None, None),
            P(None, None, "fsdp"),
            P(),
            P(None, "fsdp"),
        ),
        out_specs=P(("dp", "fsdp"), None),
        check_vma=False,
    )
```

```python
import jax
import jax.numpy as jnp
from jax import lax
from jax.experimental import pallas as pl
from jax.experimental.pallas import tpu as pltpu
from jax.sharding import PartitionSpec as P

MESH = pl.DeviceIdType.MESH
F32 = jnp.float32
BF16 = jnp.bfloat16

SINK = 3
PROTOS = 3072
EPS = 1e-06
TEMP = 0.05

N = 8
ROWS = 32
MAP = 14 * ROWS
STAGES = ((0, 512), (2048, 384), (3584, 256))
DIRECT = 1
HALF = PROTOS // 2
SLICE = 384
GRID = 64
CUBE = 8


def device(x, y, z, c):
    dp = lax.rem(x, N) * 16 + (lax.rem(z, N) // 4) * 8 + lax.rem(y, N)
    return dp, lax.rem(z, 4) * 2 + lax.rem(c, 2)


def nt(a, b):
    return lax.dot_general(a, b, (((1,), (1,)), ((), ())), preferred_element_type=F32)


def split_rows(v):
    hi = v.astype(BF16).astype(F32)
    row = lax.broadcasted_iota(jnp.int32, (16, v.shape[1]), 0)
    return jnp.where(row == 0, hi, jnp.where(row == 1, v - hi, 0.0)).astype(BF16)


def kernel(
    x_hbm, w_hbm, proj_hbm, proto_hbm, out_ref,
    wide, sib, xf, xs, acc, gath, proj, proto, prs, part, zb, ef, eh, cb, rb, fin,
    loc, sib_s, sib_r, p1_s, p1_r, p2_s, p2_r, p3_s, pr_s, pr_r, pt_s, pt_r,
    d1_s, d1_r, c_s, c_r, r_s, r_r, f_s, f_r, far,
):
    dp, fs = lax.axis_index("dp"), lax.axis_index("fsdp")
    x, y, zh = dp // 16, lax.rem(dp, 8), lax.rem(dp // 8, 2)
    zl, c = fs // 2, lax.rem(fs, 2)
    z = zh * 4 + zl
    sibling = device(x, y, z, c + 1)
    zpeer = [None] + [device(x, y, z + k, c) for k in range(1, N)]
    ypeer = [None] + [device(x, y + k, z, c) for k in range(1, N)]
    xpeer = [None] + [device(x + k, y, z, c) for k in range(1, N)]
    steps = range(0, N, 2)
    grid = [(i, j, k) for i in steps for j in steps for k in steps][1:]
    grid.sort(key=lambda step: -sum(min(a, N - a) for a in step))
    grid = [device(x + i, y + j, z + k, c) for i, j, k in grid]
    other = [a + 1 - 2 * lax.rem(a, 2) for a in (x, y, z)]
    cube, cross = [], []
    for m in (7, 6, 5, 3, 4, 2, 1):
        at = [b if m >> n & 1 else a for n, (a, b) in enumerate(zip((x, y, z), other))]
        cube.append(device(*at, c))
        cross.append(device(*at, c + 1))

    def send(src, dst, s, r, to):
        pltpu.make_async_remote_copy(
            src_ref=src, dst_ref=dst, send_sem=s, recv_sem=r, device_id=to, device_id_type=MESH
        ).start()

    def wait(ref, sem):
        pltpu.make_async_copy(ref, ref, sem).wait()

    due = []

    def drain():
        for ref, sem in due + late:
            wait(ref, sem)

    late = []
    barrier = pltpu.get_barrier_semaphore()
    near = [p[k] for ks in ((2, 6), (1, 7)) for p in (zpeer, xpeer, ypeer) for k in ks]
    for to in [sibling] + near:
        pl.semaphore_signal(barrier, inc=1, device_id=to, device_id_type=MESH)

    own = pl.ds(pl.multiple_of(zl * 64, 64), 64)
    pltpu.make_async_copy(w_hbm, gath.at[own], loc.at[0]).start()
    pltpu.make_async_copy(proto_hbm, proto, loc.at[1]).start()
    pltpu.make_async_copy(x_hbm, wide, loc.at[2]).start()
    pltpu.make_async_copy(proj_hbm, proj, loc.at[3]).start()

    pltpu.make_async_copy(proto_hbm, proto, loc.at[1]).wait()
    pw = proto[...].astype(F32)
    norm = jnp.sqrt(jnp.sum(pw * pw, axis=0, keepdims=True) + EPS)
    prs[zl] = (pw / norm).astype(BF16)

    def spread(src, slot):
        xf[...] = jnp.zeros((MAP + 96, 512), F32)
        for h in range(14):
            xf[pl.ds(48 + ROWS * h, 28), :] = src[h].astype(F32).reshape(28, 512)
        for j in range(3):
            xs[slot, j] = xf[pl.ds(14 + 2 * j, 512), :].astype(BF16)

    pltpu.make_async_copy(x_hbm, wide, loc.at[2]).wait()
    wait(gath.at[pl.ds(0, 64), :], loc.at[0])
    pltpu.make_async_copy(proj_hbm, proj, loc.at[3]).wait()

    pl.semaphore_wait(barrier, 1 + len(near))

    color = [lax.rem(x + 2 * y, 4), lax.rem(2 * x + y, 4)]

    def piece(stage, s, h, g=None, ahead=0):
        first, size = STAGES[stage]
        hue = lax.rem(color[h] + ahead, 4)
        row = s * 64 + h * 32
        rows = pl.ds(pl.multiple_of(row, 32), 32)
        if g is not None:
            rows = pl.ds(pl.multiple_of(row + 16 * g, 16), 16)
        return gath.at[rows, pl.ds(pl.multiple_of(first + hue * size, 128), size)]

    for stage in range(3):
        for h in range(2):
            mine = piece(stage, zl, h)
            send(mine, mine, p1_s, p1_r.at[stage, 0, h], zpeer[7])
            send(mine, mine, p1_s, p1_r.at[stage, 2, h], zpeer[1])
        for h in range(2):
            for g, k in ((0, 2), (1, 6)):
                mine = piece(stage, zl, h, g)
                send(mine, mine, p1_s, p1_r.at[stage, 1, h], zpeer[k])
    for h in range(2):
        mine = piece(DIRECT, zl, h, ahead=2)
        send(mine, mine, p3_s, p2_r.at[DIRECT], zpeer[7])
        send(mine, mine, p3_s, p2_r.at[DIRECT], zpeer[1])
        for g, k in ((0, 2), (1, 6)):
            mine = piece(DIRECT, zl, h, g, ahead=2)
            send(mine, mine, p3_s, p2_r.at[DIRECT], zpeer[k])
    send(wide, sib, sib_s, sib_r, sibling)
    due.append((gath.at[pl.ds(0, 48), :], p1_s))
    due.append((wide, sib_s))
    late = [(sib, sib_r)]
    for to in near:
        pl.semaphore_signal(far.at[0], inc=1, device_id=to, device_id_type=MESH)

    spread(wide, c)

    def forward(stage, k, h):
        s = lax.rem(zl + k, 4)
        full, half = (xpeer, ypeer) if h == 0 else (ypeer, xpeer)
        whole = piece(stage, s, h)
        wait(whole, p1_r.at[stage, k - 1, h])
        for to in (full[1], full[7]):
            send(whole, whole, p2_s.at[stage], p2_r.at[stage], to)
        if stage != DIRECT:
            for g, to in ((0, half[1]), (1, half[7])):
                mine = piece(stage, s, h, g)
                send(mine, mine, p2_s.at[stage], p2_r.at[stage], to)

    def prototypes():
        for to in (zpeer[1], zpeer[7]):
            send(prs.at[zl], prs.at[zl], pr_s, pr_r, to)
        for g, to in ((0, zpeer[2]), (1, zpeer[6])):
            rows = pl.ds(128 * g, 128)
            send(prs.at[zl, rows], prs.at[zl, rows], pr_s, pr_r, to)

    for stage in range(3):
        for k, h in ((1, 0), (3, 0), (1, 1), (3, 1), (2, 0), (2, 1)):
            if stage == 2 and (k, h) == (2, 0):
                prototypes()
            forward(stage, k, h)
        if stage == 0:
            pl.semaphore_wait(far.at[0], len(near))
            for to in (xpeer[2], xpeer[4], xpeer[6], cube[6]):
                pl.semaphore_signal(far.at[1], inc=1, device_id=to, device_id_type=MESH)
    for stage, (sent, came) in enumerate(((64, 64), (32, 48), (32, 32))):
        due.append((gath.at[pl.ds(0, sent), :], p2_s.at[stage]))
        late.append((gath.at[pl.ds(0, came), :], p2_r.at[stage]))
    due.append((gath.at[pl.ds(0, 16), :], p3_s))
    due.append((prs.at[pl.ds(0, 3)], pr_s))
    late.append((prs.at[pl.ds(0, 3)], pr_r))
    wait(*late.pop(0))
    spread(sib, 1 - c)

    o = lax.broadcasted_iota(jnp.int32, (256, 512), 0)
    i = lax.broadcasted_iota(jnp.int32, (256, 512), 1)
    pick = jnp.where(i == (o // 64) * 128 + 64 * c + lax.rem(o, 64), 1.0, 0.0).astype(BF16)
    for slot in range(2):
        acc[slot] = nt(xs[slot, 1, pl.ds(32, MAP), :], pick)

    pl.semaphore_wait(far.at[1], 4)
    for to in (zpeer[2], zpeer[4], zpeer[6], sibling):
        pl.semaphore_signal(far.at[2], inc=1, device_id=to, device_id_type=MESH)

    for taps in (range(4), range(4, 7), range(7, 9)):
        wait(*late.pop(0))
        for slot in range(2):
            total = acc[slot]
            for t in taps:
                r, j = divmod(t, 3)
                maps = xs[slot, j, pl.ds(32 * r, MAP), :]
                total = total + nt(maps, gath[:, pl.ds(512 * t, 512)])
            acc[slot] = total

    row32 = lax.broadcasted_iota(jnp.int32, (ROWS, 256), 0)
    row16 = lax.broadcasted_iota(jnp.int32, (16, 256), 0)
    pooled = jnp.zeros((16, 256), F32)
    for slot in range(2):
        line = jnp.sum(jnp.maximum(acc[slot].reshape(14, ROWS, 256), 0.0), axis=0)
        for b in range(2):
            keep = (lax.rem(row32, 2) == b) & (row32 < 28)
            mean = jnp.sum(jnp.where(keep, line, 0.0), axis=0, keepdims=True) / 196.0
            pooled = jnp.where(lax.rem(row16, 4) == 2 * slot + b, mean, pooled)

    weights = jnp.concatenate(
        [proj[pl.ds(pl.multiple_of(128 * a + 64 * c, 64), 64), :] for a in range(4)], axis=0
    )
    partial = jnp.dot(pooled.astype(BF16), weights, preferred_element_type=F32)
    part[0] = partial[:8]
    send(part.at[0], part.at[1], pt_s, pt_r, sibling)
    due.append((part.at[0], pt_s))
    wait(part.at[1], pt_r)
    projected = part[0] + part[1]
    norm = jnp.sqrt(jnp.sum(projected * projected, axis=1, keepdims=True) + EPS)
    embed = (projected / norm).astype(BF16).astype(F32)

    zb[0] = embed[:4].astype(BF16)
    pl.semaphore_wait(far.at[2], 4)
    for k, to in enumerate(grid):
        send(zb.at[0], zb.at[k + 1], d1_s, d1_r.at[(k + 1) // 32], to)
    due.append((zb.at[pl.ds(1, GRID - 1)], d1_s))
    wait(*late.pop(0))

    def scores(block):
        images = zb[pl.ds(32 * block, 32)].astype(F32).reshape(128, 256).astype(BF16)
        rows = pl.ds(128 * block, 128)
        for a in range(4):
            cols = pl.ds(SLICE * a, SLICE)
            e = jnp.exp(jnp.dot(images, prs[a], preferred_element_type=F32) / TEMP)
            ef[rows, cols] = e
            eh[rows, cols] = e.astype(BF16)
            column = jnp.sum(e, axis=0, keepdims=True)
            cb[0, CUBE - 1, :, cols] = column if block else column + cb[0, CUBE - 1, :, cols]

    wait(zb.at[pl.ds(32, 32)], d1_r.at[1])
    scores(1)
    wait(zb.at[pl.ds(1, 31)], d1_r.at[0])
    scores(0)

    def total_of(sums):
        total = sums[0]
        for k in range(1, CUBE):
            total = total + sums[k]
        return total

    for sweep in range(SINK - 1):
        sums = cb.at[sweep]
        for k, to in enumerate(cube):
            send(sums.at[CUBE - 1], sums.at[k], c_s.at[sweep], c_r.at[sweep], to)
        due.append((sums.at[pl.ds(0, CUBE - 1)], c_s.at[sweep]))
        if sweep == 0:
            fin[0] = ef[pl.ds(0, 8), :][:4]
            send(fin.at[0], fin.at[1], f_s, f_r, sibling)
            due.append((fin.at[0], f_s))
        wait(sums.at[pl.ds(0, CUBE - 1)], c_r.at[sweep])
        v = 1.0 / total_of(sums)
        vv = split_rows(v)
        s = nt(vv, eh[...])
        rb[sweep, 0] = s[0:1] + s[1:2]
        send(rb.at[sweep, 0], rb.at[sweep, 1], r_s.at[sweep], r_r.at[sweep], sibling)
        due.append((rb.at[sweep, 0], r_s.at[sweep]))
        wait(rb.at[sweep, 1], r_r.at[sweep])
        uu = split_rows(1.0 / (rb[sweep, 0] + rb[sweep, 1]))
        s = jnp.dot(uu, eh[...], preferred_element_type=F32)
        cb[sweep + 1, CUBE - 1] = s[0:1] + s[1:2]

    sums, theirs = cb.at[2], cb.at[3]
    for k in range(CUBE - 1):
        send(sums.at[CUBE - 1], sums.at[k], c_s.at[2], c_r.at[2], cube[k])
        send(sums.at[CUBE - 1], theirs.at[k], c_s.at[3], c_r.at[3], cross[k])
    send(sums.at[CUBE - 1], theirs.at[CUBE - 1], c_s.at[3], c_r.at[3], sibling)
    due.append((sums.at[pl.ds(0, CUBE - 1)], c_s.at[2]))
    due.append((theirs, c_s.at[3]))
    wait(fin.at[1], f_r)
    wait(sums.at[pl.ds(0, CUBE - 1)], c_r.at[2])
    wait(theirs, c_r.at[3])
    here = fin[0] * (1.0 / total_of(sums))
    there = fin[1] * (1.0 / total_of(theirs))
    even = jnp.where(c == 0, here, there)
    odd = jnp.where(c == 0, there, here)
    rows = jnp.sum(even, axis=1, keepdims=True) + jnp.sum(odd, axis=1, keepdims=True)
    scale = PROTOS / rows
    even, odd = even * scale, odd * scale
    first = 2 * c
    rowc = lax.broadcasted_iota(jnp.int32, (4, SLICE), 0)
    for b in range(2):
        for a in range(4):
            for half, codes in ((0, even), (1, odd)):
                mine = jnp.where(rowc == first + b, codes[:, SLICE * a : SLICE * (a + 1)], 0.0)
                out_ref[pl.ds(b, 1), pl.ds(SLICE * (2 * a + half), SLICE)] = jnp.sum(
                    mine, axis=0, keepdims=True
                )

    drain()


def shards(features, conv_weight, proj_weight, prototypes):
    maps = jnp.transpose(features[:, :, :, 0, :], (1, 2, 0, 3))
    weight = jnp.transpose(conv_weight[0])
    dma = pltpu.SemaphoreType.DMA
    return pl.pallas_call(
        kernel,
        out_shape=jax.ShapeDtypeStruct((2, PROTOS), F32),
        in_specs=[pl.BlockSpec(memory_space=pltpu.HBM)] * 4,
        out_specs=pl.BlockSpec(memory_space=pltpu.VMEM),
        scratch_shapes=[
            pltpu.VMEM((14, 14, 2, 512), BF16),
            pltpu.VMEM((14, 14, 2, 512), BF16),
            pltpu.VMEM((MAP + 96, 512), F32),
            pltpu.VMEM((2, 3, 512, 512), BF16),
            pltpu.VMEM((2, MAP, 256), F32),
            pltpu.VMEM((256, 4608), BF16),
            pltpu.VMEM((512, 256), BF16),
            pltpu.VMEM((256, SLICE), BF16),
            pltpu.VMEM((4, 256, SLICE), BF16),
            pltpu.VMEM((2, 8, 256), F32),
            pltpu.VMEM((GRID, 4, 256), BF16),
            pltpu.VMEM((256, HALF), F32),
            pltpu.VMEM((256, HALF), BF16),
            pltpu.VMEM((SINK + 1, CUBE, 1, HALF), F32),
            pltpu.VMEM((SINK - 1, 2, 1, 256), F32),
            pltpu.VMEM((2, 4, HALF), F32),
            dma((4,)),
            dma, dma,
            dma, dma((3, 3, 2)),
            dma((3,)), dma((3,)), dma,
            dma, dma,
            dma, dma,
            dma, dma((2,)),
            dma((SINK + 1,)), dma((SINK + 1,)),
            dma((SINK - 1,)), dma((SINK - 1,)),
            dma, dma,
            pltpu.SemaphoreType.REGULAR((3,)),
        ],
        compiler_params=pltpu.CompilerParams(
            collective_id=0, has_side_effects=True, vmem_limit_bytes=48000 * 1024
        ),
    )(*[pltpu.with_memory_space_constraint(a, pltpu.HBM) for a in (maps, weight, proj_weight, prototypes)])


def solution(mesh):
    return jax.shard_map(
        shards,
        mesh=mesh,
        in_specs=(
            P(("dp", "fsdp"), None, None, None, None),
            P(None, None, "fsdp"),
            P(),
            P(None, "fsdp"),
        ),
        out_specs=P(("dp", "fsdp"), None),
        check_vma=False,
    )
```
